32 devices in a mesh: groups: 2 (over x), tm: 16 (over z, y, core).
Axes of the slice: x: 2, y: 2, z: 4, core: 2. Of those that a mesh axis runs over, the one named last changes fastest.
Arguments:
- signal: float32 [2, 8192], P('groups', 'tm'), parts along dimension 0, may hold values from -6 to 6
- codes: bfloat16 [2, 1024, 8192], P('groups', None, 'tm'), parts along dimension 0, may hold values from -6 to 6
- dictionary: float32 [1024, 512], P('tm'), may hold values from -6 to 6
- thresholds: float32 [1024], replicated, may hold values from 0.02 to 0.2
Outputs:
- codes_out: bfloat16 [2, 1024, 8192], P('groups', None, 'tm'), parts along dimension 0
- dictionary_out: float32 [2048, 512], P(('groups', 'tm')), parts along dimension 0
- residual_out: float32 [2, 8192], P('groups', 'tm'), parts along dimension 0
The draws below stay inside these ranges and needn't reach their ends.
There are 2 independent parts, one for each index of `groups`. The reference program is written for one: setup_inputs(seed, part) draws one part's arguments, and reference() takes and returns one part's arrays. A program takes and returns all parts, laid end to end along the dimension named above; an argument that names none is the same for every part. Nothing has to cross between parts.
All inputs are finite; a program needn't handle non-finite values.
Results may differ from the reference program's by a relative error of at most 0.0072.
Values may be sent and summed in bfloat16 or wider, within the bound.
A program may use at most 64 MiB of HBM per device.

```python
import math
import jax
import jax.numpy as jnp
from jax import lax

C = 1
K = 1024
L = 512
ITERS = 2
T_SIZE = 8192


def raised(values, key, source, target, parts, factor):
    def block_of(axis_at):
        return (jnp.arange(values.shape[axis_at]) // (values.shape[axis_at] // parts)).reshape((-1,) + (1,) * (values.ndim - 1 - axis_at))

    near = jax.random.permutation(key, parts)[block_of(target)]
    second = (block_of(target) + parts // 2) % parts
    return jnp.where((block_of(source) == near) | (block_of(source) == second), factor * values, values)


def level_of(key, shape, shards, low, high):
    level, own = 1.0, jax.random.fold_in(key, 6)
    for dim, shards_of in shards:
        steps = jnp.exp(jax.random.uniform(jax.random.fold_in(own, dim), (shards_of,), jnp.float32, low / len(shards), high / len(shards)))
        level = level * jnp.repeat(steps, shape[dim] // shards_of).reshape([-1 if axis == dim else 1 for axis in range(len(shape))])
    return level


def scatter_about(key, extent, deviation, most, shards=(), kind=jnp.bfloat16):
    level = level_of(key, extent, shards, -0.22, 0.18) if shards else 1.0
    values = jax.random.normal(key, extent, jnp.float32) * deviation * level
    return jnp.minimum(jnp.maximum(values, -most), most).astype(kind)


def noise_with(key, extent, width, limit, pieces, heavy, dtype=jnp.bfloat16):
    drawn = width * jax.random.normal(key, extent, jnp.float32)
    if pieces:
        drawn = drawn * level_of(key, extent, pieces, -0.22, 0.18)
    return jnp.clip(raised(drawn, jax.random.fold_in(key, 3), *heavy), -limit, limit).astype(dtype)


def setup_inputs(seed: int = 0, part: int = 0) -> dict:
    keys = jax.random.split(jax.random.key(seed), 5)
    own_keys = jax.random.split(jax.random.fold_in(keys[4], part), 5)
    signal = scatter_about(own_keys[0], (C, T_SIZE), 1.0, 6.0, ((1, 16),), jnp.float32)
    codes = noise_with(own_keys[1], (C, K, T_SIZE), 1.0, 6.0, ((2, 16),), (2, 1, 16, 2.0))
    dictionary = scatter_about(keys[2], (K, L), 1.0, 6.0, ((0, 16),), jnp.float32)
    thresholds = jnp.clip(jnp.exp(jax.random.uniform(keys[3], (K,), jnp.float32, math.log(0.02), math.log(0.2))), 0.02, 0.2)
    return {"signal": signal, "codes": codes, "dictionary": dictionary, "thresholds": thresholds}


CODE_STEP = 6.0
EPSILON = 1e-06

def round_keep(values):
    return lax.optimization_barrier(values.astype(jnp.bfloat16)).astype(jnp.float32)

def reference(signal, codes, dictionary, thresholds):
    factor = (K * L) ** (-0.5)
    current = codes.astype(jnp.float32)
    atoms_now = dictionary
    residual = signal
    numbers = ('NCH', 'OIH', 'NCH')
    for iteration in range(ITERS):
        dict_b = round_keep(atoms_now)
        codes_b = round_keep(current)
        rebuilt = lax.conv_general_dilated(codes_b, dict_b[None, :, ::-1], (1,), [(L - 1, 0)], dimension_numbers=numbers, precision=lax.Precision.HIGHEST)[:, 0, :]
        residual = signal - factor * rebuilt
        rounded = round_keep(residual)
        matched = lax.conv_general_dilated(rounded[:, None, :], dict_b[:, None, :], (1,), [(0, L - 1)], dimension_numbers=numbers, precision=lax.Precision.HIGHEST)
        gradient = factor * lax.conv_general_dilated(rounded[None], jnp.transpose(codes_b, (1, 0, 2)), (1,), [(0, L - 1)], dimension_numbers=numbers, precision=lax.Precision.HIGHEST)[0]
        shrink = current + CODE_STEP * factor * matched
        cutoff = CODE_STEP * thresholds[None, :, None]
        current = jnp.sign(shrink) * jnp.maximum(jnp.abs(shrink) - cutoff, 0.0)
        updated = atoms_now + gradient
        atoms_now = updated / jnp.sqrt(lax.optimization_barrier(jnp.mean(updated * updated, axis=1, keepdims=True)) + EPSILON)
    return (current.astype(jnp.bfloat16), atoms_now, residual)
```

```python
import functools

import jax
import jax.numpy as jnp
from jax import lax
from jax.experimental import pallas as pl
from jax.experimental.pallas import tpu as pltpu
from jax.sharding import PartitionSpec as P

ITERS = 2
CODE_STEP = 6.0
EPSILON = 1e-06
LANES = 128
MESH = pl.DeviceIdType.MESH
BF16, F32 = jnp.bfloat16, jnp.float32
PIECES = 2


def pieces_of(rows):
    return max(1, min(PIECES, rows // 16))


def rolled(x, shift):
    width = x.shape[1]
    shift = shift % width
    return x if shift == 0 else pltpu.roll(x, shift, 1)


def skew_total(lagged):
    lag_count, time_len = lagged.shape
    width = lag_count + time_len
    total = None
    for a in range(LANES // 8):
        part = None
        for b in range(lag_count // LANES):
            block = lagged[pl.ds(b * LANES + a * 8, 8), :]
            pieces = [block]
            if b:
                pieces.insert(0, jnp.zeros((8, b * LANES), F32))
            if width - b * LANES - time_len:
                pieces.append(jnp.zeros((8, width - b * LANES - time_len), F32))
            block = jnp.concatenate(pieces, axis=1)
            part = block if part is None else part + block
        part = rolled(part, 8 * a)
        total = part if total is None else total + part
    out = total[0:1, :]
    for r in range(1, 8):
        out = out + rolled(total, r)[r : r + 1, :]
    return out


def fill_frames(frames, extended):
    lag_count = frames.shape[1]
    width = extended.shape[1]
    halves = frames.shape[0] // lag_count
    wide = jnp.broadcast_to(extended, (8, width))
    row = lax.broadcasted_iota(jnp.int32, (8, width), 0)
    base = wide
    for r in range(1, 8):
        base = jnp.where(row == r, rolled(wide, width - r), base)
    for a in range(LANES // 16):
        low, high = rolled(base, width - 16 * a), rolled(base, width - 16 * a - 8)
        both = jnp.concatenate([low, high], axis=0).astype(BF16)
        for half in range(halves):
            for b in range(lag_count // LANES):
                at = half * lag_count + b * LANES
                frames[pl.ds(at + a * 16, 16), :] = both[:, at : at + lag_count]


def kernel(
    n, signal_hbm, codes_hbm, dictionary_hbm, thresholds_hbm,
    codes_out, atoms_out, residual_out,
    atoms_ref, signal_ref, dictionary_ref, thresholds_ref, cutoffs_all, cutoffs, codes_b, current, atoms_b, lagged,
    frames, grad, keep, extended_ref, part_send, from_partner, from_previous, from_following,
    y_send, y_recv, z_send, z_recv,
    local_sem, send_sem, whole_r, halo_r, az_r, over_r, gy_r, gz_r,
):
    rows, lag_count = dictionary_ref.shape
    nz, _, _, width = codes_b.shape
    atom_count = 4 * nz * rows
    factor = (atom_count * lag_count) ** (-0.5)
    pieces = pieces_of(rows)
    part = rows // pieces
    me = lax.axis_index("tm")
    core, y, z = me % 2, (me // 2) % 2, me // 4
    chip, chips = me // 2, n // 2

    def index_of(zz, yy, cc):
        return (zz * 2 + yy) * 2 + cc

    partner = index_of(z, y, 1 - core)
    across = index_of(z, 1 - y, core)
    upper = (z * 2) // nz

    def layer_at(d):
        if d == nz - 1:
            return z
        fall, rise = nz - 1 - d, d
        fall = fall - (z - fall + nz) // nz
        rise = rise + (rise - z + nz) // nz
        return upper * rise + (1 - upper) * fall

    layers = [layer_at(d) for d in range(nz)]
    others = range(nz - 1)
    def copy_to(src, dst, send, recv_sem, target):
        return pltpu.make_async_remote_copy(
            src_ref=src, dst_ref=dst, send_sem=send_sem.at[send], recv_sem=recv_sem,
            device_id={"tm": target}, device_id_type=MESH,
        )

    def arrived(ref, recv_sem):
        pltpu.make_async_copy(ref, ref, recv_sem).wait()

    sent = []

    def start(copy, when=None):
        if when is None:
            copy.start()
        else:
            pl.when(when)(copy.start)
        sent.append((copy, when))

    def lanes_of(cc):
        return pl.ds(pl.multiple_of(cc * lag_count, LANES), lag_count)

    def slab(p):
        return pl.ds(p * part, part)

    own = lanes_of(core)
    loads = [
        pltpu.make_async_copy(dictionary_hbm, dictionary_ref, local_sem.at[0]),
        pltpu.make_async_copy(signal_hbm, signal_ref, local_sem.at[1]),
        pltpu.make_async_copy(thresholds_hbm, thresholds_ref, local_sem.at[2]),
        pltpu.make_async_copy(codes_hbm.at[:, :, core], codes_b.at[:, :, :, own], local_sem.at[3]),
    ]
    for load in loads:
        load.start()

    barrier = pltpu.get_barrier_semaphore()
    for target in [partner, across] + [index_of(layers[d], y, core) for d in others]:
        pl.semaphore_signal(barrier, inc=1, device_id={"tm": target}, device_id_type=MESH)

    loads[0].wait()
    atoms_ref[...] = dictionary_ref[...]
    atoms_b[0, z, y] = dictionary_ref[...].astype(BF16)
    pl.semaphore_wait(barrier, 2 + nz - 1)

    def piece(it, zz, yy, p):
        return atoms_b.at[it, zz, yy, slab(p), :]

    def along(it, zz, p, target):
        held = piece(it, zz, y, p)
        return copy_to(held, held, 0, az_r.at[zz, p], index_of(target, y, core))

    def over(it, zz, p):
        held = piece(it, zz, y, p)
        return copy_to(held, held, 1, over_r.at[0], across)

    def offer(it, p):
        for d in others:
            start(along(it, z, p, layers[d]))
        start(over(it, z, p))

    def landed(it, zz, p):
        arrived(piece(it, zz, y, p), az_r.at[zz, p])
        over(it, zz, p).start()

    def gather(it):
        for p in range(pieces):
            for hops in range(1, nz):
                pl.when(z - hops >= 0)(functools.partial(landed, it, z - hops, p))
                pl.when(z + hops < nz)(functools.partial(landed, it, z + hops, p))
            for d in others:
                sent.append((over(it, layers[d], p), None))
        theirs = atoms_b.at[it, :, 1 - y]
        arrived(theirs, over_r.at[0])

    for p in range(pieces):
        offer(0, p)
    start(copy_to(codes_hbm.at[:, :, 1 - core], codes_b.at[:, :, :, own], 2, whole_r.at[0], partner))
    loads[2].wait()
    cutoffs_all[...] = CODE_STEP * jnp.broadcast_to(thresholds_ref[...], (8, atom_count)).T[:, 0:1]
    for zz in range(nz):
        for yy in range(2):
            at = pl.multiple_of(index_of(zz, yy, core) * rows, rows)
            cutoffs[zz, yy] = cutoffs_all[pl.ds(at, rows), :]
    loads[1].wait()

    for it in range(ITERS):
        last = it == ITERS - 1
        gather(it)
        if it == 0:
            loads[3].wait()
            arrived(codes_b.at[:, :, :, lanes_of(1 - core)], whole_r.at[0])
        lagged[...] = lax.dot_general(
            atoms_b[it].reshape(2 * nz * rows, lag_count), codes_b[...].reshape(2 * nz * rows, width),
            (((0,), (0,)), ((), ())), preferred_element_type=F32,
        )
        part_send[it] = -factor * skew_total(lagged)
        part_send[it, :, own] += signal_ref[...]

        start(copy_to(part_send.at[it], from_partner.at[it], 3, halo_r.at[it, 0], partner))
        for cc in range(2):
            start(
                copy_to(
                    part_send.at[it, :, pl.ds(width, lag_count)], from_previous.at[it, core],
                    3, halo_r.at[it, 1], 2 * (chip + 1) + cc,
                ),
                chip < chips - 1,
            )
            start(
                copy_to(
                    part_send.at[it, :, pl.ds(0, lag_count)], from_following.at[it, core],
                    3, halo_r.at[it, 2], 2 * (chip - 1) + cc,
                ),
                chip > 0,
            )

        @pl.when(chip == 0)
        def _():
            from_previous[it] = jnp.zeros_like(from_previous[it])

        @pl.when(chip == chips - 1)
        def _():
            from_following[it] = jnp.zeros_like(from_following[it])

        arrived(from_partner.at[it], halo_r.at[it, 0])

        @pl.when(chip > 0)
        def _():
            arrived(from_previous.at[it], halo_r.at[it, 1])

        @pl.when(chip < chips - 1)
        def _():
            arrived(from_following.at[it], halo_r.at[it, 2])

        total = part_send[it] + from_partner[it]
        head = total[:, :lag_count] + (from_previous[it, 0] + from_previous[it, 1])
        tail = total[:, width:] + (from_following[it, 0] + from_following[it, 1])
        residual = jnp.concatenate([head, total[:, lag_count:width], tail], axis=1)
        lane = lax.broadcasted_iota(jnp.int32, residual.shape, 1)
        held = width + lag_count * jnp.minimum(chips - 1 - chip, 1)
        residual = jnp.where(lane < held, residual, 0.0)
        if last:
            extended_ref[...] = residual
            residual_store = pltpu.make_async_copy(extended_ref.at[:, own], residual_out, local_sem.at[1])
            residual_store.start()
        fill_frames(frames, residual.astype(BF16).astype(F32))

        order = range(nz)
        column = (nz * rows, width)
        crossing = jnp.dot(codes_b[:, 1 - y].reshape(column), frames[...], preferred_element_type=F32)
        y_send[it] = crossing.reshape(nz, rows, lag_count).astype(BF16)

        def y_copy(d, p):
            lay = layers[d]
            return copy_to(y_send.at[it, lay, slab(p), :], y_recv.at[it, lay, slab(p), :], 4, gy_r.at[d, p], across)

        def z_copy(lay, p):
            return copy_to(
                z_send.at[it, lay, slab(p), :], z_recv.at[it, z, slab(p), :], 5, gz_r.at[z, p], index_of(lay, y, core)
            )

        for p in range(pieces):
            for d in order:
                start(y_copy(d, p))
        grad[...] = jnp.dot(
            codes_b[:, y].reshape(column), frames[...], preferred_element_type=F32
        ).reshape(nz, rows, lag_count)

        def advance(yy, half):
            picked = pl.ds(half * lag_count, lag_count)
            matched = jnp.dot(
                atoms_b[it, :, yy].reshape(nz * rows, lag_count), frames[picked, :], preferred_element_type=F32
            )
            store = (slice(None), yy, slice(None), picked)
            before = codes_b[store].astype(F32) if it == 0 else current[store]
            shrink = before + (CODE_STEP * factor) * matched.reshape(nz, rows, lag_count)
            cutoff = cutoffs[:, yy]
            after = shrink - jnp.minimum(jnp.maximum(shrink, -cutoff), cutoff)
            if not last:
                current[store] = after
            codes_b[store] = after.astype(BF16)

        for yy in range(2):
            for half in range(2):
                advance(yy, half)
        if last:
            store = pltpu.make_async_copy(codes_b.at[:, :, :, own], codes_out.at[:, :, core], local_sem.at[0])
            start(copy_to(codes_b.at[:, :, :, lanes_of(1 - core)], codes_out.at[:, :, core], 2, whole_r.at[1], partner))
            store.start()

        def atoms_store(p):
            return pltpu.make_async_copy(atoms_ref.at[slab(p), :], atoms_out.at[slab(p), :], local_sem.at[2 + p])

        def summed(lay, p):
            return grad[lay, slab(p), :] + y_recv[it, lay, slab(p), :].astype(F32)

        def finish(p):
            total = keep[slab(p), :]
            for d in others:
                arrived(z_recv.at[it, layers[d], slab(p), :], gz_r.at[layers[d], p])
                total = total + z_recv[it, layers[d], slab(p), :].astype(F32)
            updated = atoms_ref[slab(p), :] + factor * total
            fresh = updated / jnp.sqrt(jnp.mean(updated * updated, axis=1, keepdims=True) + EPSILON)
            atoms_ref[slab(p), :] = fresh
            if last:
                atoms_store(p).start()
            else:
                atoms_b[it + 1, z, y, slab(p), :] = fresh.astype(BF16)
                offer(it + 1, p)

        for p in range(pieces):
            for d in order:
                arrived(y_recv.at[it, layers[d], slab(p), :], gy_r.at[d, p])
                if d == nz - 1:
                    keep[slab(p), :] = summed(layers[d], p)
                else:
                    z_send[it, layers[d], slab(p), :] = summed(layers[d], p).astype(BF16)
                    start(z_copy(layers[d], p))
                if d == nz - 2 and p:
                    finish(p - 1)
        finish(pieces - 1)

    arrived(codes_out.at[:, :, 1 - core], whole_r.at[1])
    for store in [store, residual_store] + [atoms_store(p) for p in range(pieces)]:
        store.wait()
    for copy, when in sent:
        if when is None:
            copy.wait_send()
        else:
            pl.when(when)(copy.wait_send)


def on_device(n, signal, codes, dictionary, thresholds):
    _, atom_count, time_len = codes.shape
    rows, lag_count = dictionary.shape
    nz = n // 4
    width = 2 * time_len
    pieces = pieces_of(rows)
    vmem, dma = pltpu.VMEM, pltpu.SemaphoreType.DMA
    outside = pl.BlockSpec(memory_space=pltpu.HBM)
    piece = (rows, lag_count)
    split = (nz, 2, 2, rows, time_len)
    given = [
        pltpu.with_memory_space_constraint(x, pltpu.HBM)
        for x in (signal, codes.reshape(split), dictionary, thresholds[None, :])
    ]
    made = tuple(
        pl.pallas_call(
            functools.partial(kernel, n),
            name="learn",
            out_shape=(vmem(split, BF16), vmem(piece, F32), vmem(signal.shape, F32)),
            in_specs=[outside] * 4,
            out_specs=(pl.BlockSpec(memory_space=pl.ANY),) * 3,
            scratch_shapes=[
                vmem(piece, F32),
                vmem(signal.shape, F32),
                vmem(piece, F32),
                vmem((1, atom_count), F32),
                vmem((atom_count, 1), F32),
                vmem((nz, 2, rows, 1), F32),
                vmem((nz, 2, rows, width), BF16),
                vmem((nz, 2, rows, width), F32),
                vmem((ITERS, nz, 2, *piece), BF16),
                vmem((lag_count, width), F32),
                vmem((width, lag_count), BF16),
                vmem((nz, *piece), F32),
                vmem(piece, F32),
                vmem((1, width + lag_count), F32),
                vmem((ITERS, 1, width + lag_count), F32),
                vmem((ITERS, 1, width + lag_count), F32),
                vmem((ITERS, 2, 1, lag_count), F32),
                vmem((ITERS, 2, 1, lag_count), F32),
                vmem((ITERS, nz, *piece), BF16),
                vmem((ITERS, nz, *piece), BF16),
                vmem((ITERS, nz, *piece), BF16),
                vmem((ITERS, nz, *piece), BF16),
                dma((4,)),
                dma((6,)),
                dma((2,)),
                dma((ITERS, 3)),
                dma((nz, pieces)),
                dma((1,)),
                dma((nz, pieces)),
                dma((nz, pieces)),
            ],
            compiler_params=pltpu.CompilerParams(
                collective_id=0, has_side_effects=True, vmem_limit_bytes=48_000_000
            ),
        )(*given)
    )

    def publish(codes_ref, atoms_ref, residual_ref, codes_out, atoms_out, residual_out, sems):
        pairs = [(codes_ref, codes_out), (atoms_ref, atoms_out), (residual_ref, residual_out)]
        puts = [pltpu.make_async_copy(src, dst, sems.at[i]) for i, (src, dst) in enumerate(pairs)]
        for put in puts:
            put.start()
        for put in puts:
            put.wait()

    codes_out, atoms_out, residual_out = pl.pallas_call(
        publish,
        name="publish",
        out_shape=tuple(jax.ShapeDtypeStruct(x.shape, x.dtype) for x in made),
        in_specs=[pl.BlockSpec(memory_space=pl.ANY)] * 3,
        out_specs=(outside,) * 3,
        scratch_shapes=[dma((3,))],
        compiler_params=pltpu.CompilerParams(vmem_limit_bytes=1_000_000),
    )(*made)
    return codes_out.reshape(codes.shape), atoms_out, residual_out


def solution(mesh):
    return jax.shard_map(
        functools.partial(on_device, mesh.shape["tm"]),
        mesh=mesh,
        in_specs=(P("groups", "tm"), P("groups", None, "tm"), P("tm", None), P()),
        out_specs=(P("groups", None, "tm"), P(("groups", "tm"), None), P("groups", "tm")),
        check_vma=False,
    )
```

```python
import functools

import jax
import jax.numpy as jnp
from jax import lax
from jax.experimental import pallas as pl
from jax.experimental.pallas import tpu as pltpu
from jax.sharding import PartitionSpec as P

ITERS = 2
CODE_STEP = 6.0
EPSILON = 1e-06
LANES = 128
MESH = pl.DeviceIdType.MESH
BF16, F32 = jnp.bfloat16, jnp.float32
PIECES = 2


def pieces_of(rows):
    return max(1, min(PIECES, rows // 16))


def rolled(x, shift):
    width = x.shape[1]
    shift = shift % width
    return x if shift == 0 else pltpu.roll(x, shift, 1)


def skew_total(lagged):
    lag_count, time_len = lagged.shape
    width = lag_count + time_len
    total = None
    for a in range(LANES // 8):
        part = None
        for b in range(lag_count // LANES):
            block = lagged[pl.ds(b * LANES + a * 8, 8), :]
            pieces = [block]
            if b:
                pieces.insert(0, jnp.zeros((8, b * LANES), F32))
            if width - b * LANES - time_len:
                pieces.append(jnp.zeros((8, width - b * LANES - time_len), F32))
            block = jnp.concatenate(pieces, axis=1)
            part = block if part is None else part + block
        part = rolled(part, 8 * a)
        total = part if total is None else total + part
    for step in (4, 2, 1):
        total = total + pltpu.roll(rolled(total, step), 8 - step, 0)
    return total[0:1, :]


def fill_frames(frames, extended):
    lag_count, length = frames.shape
    width = extended.shape[1]
    base = jnp.broadcast_to(extended, (8, width))
    row = lax.broadcasted_iota(jnp.int32, (8, width), 0)
    for step in (1, 2, 4):
        base = jnp.where((row // step) % 2 == 1, rolled(base, width - step), base)
    for a in range(LANES // 16):
        low, high = rolled(base, width - 16 * a), rolled(base, width - 16 * a - 8)
        both = jnp.concatenate([low, high], axis=0).astype(BF16)
        for b in range(lag_count // LANES):
            frames[pl.ds(b * LANES + a * 16, 16), :] = both[:, b * LANES : b * LANES + length]


def kernel(
    n, signal_hbm, codes_hbm, dictionary_hbm, thresholds_hbm,
    codes_out, atoms_out, residual_out,
    atoms_ref, rest, signal_ref, thresholds_ref, cutoffs_all, cutoffs, codes_b, current, atoms_b, codes_main, lagged,
    frames, grad, extended_ref, shares, from_previous, from_following,
    sum_send, sum_recv, last_recv,
    local_sem, send_sem, codes_r, halo_r, line_r, sum_r, full_r, out_r,
):
    rows, lag_count = dictionary_hbm.shape
    _, lines, _, length = codes_main.shape
    team = 8
    half = lag_count // 2
    width = length - half
    atom_count = lines * team * rows
    factor = (atom_count * lag_count) ** (-0.5)
    slab_len = width // 4
    pieces = pieces_of(rows)
    part = rows // pieces
    me = lax.axis_index("tm")
    pos, group = me % team, me // team
    core, chip = pos % 2, pos // 2

    def flipped(bits):
        at = 0
        for bit in (4, 2, 1):
            one = (pos // bit) % 2
            at = at + bit * ((1 - one) if bits & bit else one)
        return at

    def member(at, group_of=group):
        return group_of * team + at

    partner = member(flipped(1))
    mates = [(group + k) % lines for k in range(1, lines)]

    def copy_to(src, dst, send, recv_sem, target):
        return pltpu.make_async_remote_copy(
            src_ref=src, dst_ref=dst, send_sem=send_sem.at[send], recv_sem=recv_sem,
            device_id={"tm": target}, device_id_type=MESH,
        )

    def arrived(ref, recv_sem):
        pltpu.make_async_copy(ref, ref, recv_sem).wait()

    sent = []

    def start(copy, when=None):
        if when is None:
            copy.start()
        else:
            pl.when(when)(copy.start)
        sent.append((copy, when))

    def lanes_of(at):
        return pl.ds(pl.multiple_of(at * lag_count, LANES), lag_count)

    def slab(p):
        return pl.ds(p * part, part)

    loads = [
        pltpu.make_async_copy(dictionary_hbm, atoms_ref.at[group], local_sem.at[0]),
        pltpu.make_async_copy(signal_hbm, signal_ref, local_sem.at[1]),
        pltpu.make_async_copy(thresholds_hbm, thresholds_ref, local_sem.at[2]),
        pltpu.make_async_copy(codes_hbm.at[:, chip, core], codes_main.at[0, :, :, lanes_of(pos)], codes_r.at[0]),
        pltpu.make_async_copy(codes_hbm.at[:, :, core], codes_b.at[:, :, :, lanes_of(core)], codes_r.at[1]),
    ]
    for load in loads:
        load.start()

    barrier = pltpu.get_barrier_semaphore()

    def greet(target):
        pl.semaphore_signal(barrier, inc=1, device_id={"tm": target}, device_id_type=MESH)

    for bits in range(1, team):
        greet(member(flipped(bits)))
    for mate in mates:
        greet(member(pos, mate))

    loads[0].wait()
    atoms_b[0, group, chip] = atoms_ref[group].astype(BF16)
    rest[group] = (atoms_ref[group] - atoms_b[0, group, chip].astype(F32)).astype(BF16)
    pl.semaphore_wait(barrier, team - 1 + lines - 1)

    for mate in mates:
        held = atoms_b.at[0, group, chip]
        start(copy_to(held, held, 0, line_r.at[0], member(pos, mate)))
    for bits in (7, 6, 3, 2, 5, 4, 1):
        at = flipped(bits)
        start(
            copy_to(
                codes_hbm.at[:, at // 2, at % 2], codes_main.at[0, :, :, lanes_of(pos)], 1, codes_r.at[0], member(at)
            )
        )
    start(copy_to(codes_hbm.at[:, :, 1 - core], codes_b.at[:, :, :, lanes_of(core)], 1, codes_r.at[1], partner))
    codes_main[0, :, :, pl.ds(width, half)] = jnp.zeros((lines, rows, half), BF16)
    codes_main[1, :, :, pl.ds(0, half)] = jnp.zeros((lines, rows, half), BF16)
    loads[2].wait()
    cutoffs_all[...] = CODE_STEP * jnp.broadcast_to(thresholds_ref[...], (8, atom_count)).T[:, 0:1]
    for i in range(lines):
        for u in range(team // 2):
            at = pl.multiple_of((i * team + 2 * u + core) * rows, rows)
            cutoffs[i, u] = cutoffs_all[pl.ds(at, rows), :]
    loads[1].wait()

    def share_atoms(it, p):
        held = atoms_b.at[it, :, chip, slab(p), :]
        for bits in (6, 2, 4):
            start(copy_to(held, held, 0, full_r.at[it], member(flipped(bits))))

    def shrunk(before, matched, cutoff):
        shrink = before + (CODE_STEP * factor) * matched
        return shrink - jnp.minimum(jnp.maximum(shrink, -cutoff), cutoff)

    def product(atoms, at):
        low = jnp.dot(atoms[:, :half], frames[:, pl.ds(at, lag_count)], preferred_element_type=F32)
        return low + jnp.dot(atoms[:, half:], frames[:, pl.ds(at + half, lag_count)], preferred_element_type=F32)

    def advance(it, side):
        at = pl.multiple_of((2 * chip + side) * lag_count, LANES)
        for i in range(lines):
            matched = product(atoms_b[it, i].reshape(4 * rows, lag_count), at)
            store = (i, slice(None), slice(None), lanes_of(side))
            before = codes_b[store].astype(F32) if it == 0 else current[store]
            after = shrunk(before, matched.reshape(4, rows, lag_count), cutoffs[i])
            if it < ITERS - 1:
                current[store] = after
            codes_b[store] = after.astype(BF16)

    def advance_main(it):
        atoms = atoms_b[it, :, chip].reshape(lines * rows, lag_count)
        cutoff = cutoffs[:, chip]
        for i in range(team):
            store = (slice(None), slice(None), pl.ds(i * lag_count, lag_count))
            matched = product(atoms, i * lag_count).reshape(lines, rows, lag_count)
            if it == 0:
                before = codes_main[(0, *store)].astype(F32)
            after = shrunk(before, matched, cutoff).astype(BF16)
            codes_main[(0, *store)] = after
            codes_main[1, :, :, pl.ds(i * lag_count + half, lag_count)] = after

    early = pieces // 2

    for it in range(ITERS):
        last = it == ITERS - 1
        if it == 0:
            arrived(atoms_b.at[0, pl.ds(0, lines - 1), 0], line_r.at[0])
            arrived(codes_main.at[0, :, :, pl.ds(0, width)], codes_r.at[0])
            for mate in mates:
                start(copy_to(rest.at[group], rest.at[group], 0, line_r.at[1], member(pos, mate)))
            codes_main[1, :, :, pl.ds(half, width)] = codes_main[0, :, :, pl.ds(0, width)]
        atoms = atoms_b[it, :, chip].reshape(lines * rows, lag_count)
        lagged[...] = lax.dot_general(
            jnp.concatenate([atoms[:, :half], atoms[:, half:]], axis=0),
            codes_main[...].reshape(2 * lines * rows, length),
            (((0,), (0,)), ((), ())), preferred_element_type=F32,
        )
        shares[it, pos] = -factor * skew_total(lagged)
        shares[it, pos, :, lanes_of(pos)] += signal_ref[...]

        for bits in (7, 6, 3, 2, 5, 4, 1):
            held = shares.at[it, pos]
            start(copy_to(held, held, 2, halo_r.at[it, 0], member(flipped(bits))))
        for at in range(team):
            start(
                copy_to(
                    shares.at[it, pos, :, pl.ds(width, lag_count)], from_previous.at[it, pos],
                    2, halo_r.at[it, 1], member(at, group + 1),
                ),
                group < lines - 1,
            )
            start(
                copy_to(
                    shares.at[it, pos, :, pl.ds(0, lag_count)], from_following.at[it, pos],
                    2, halo_r.at[it, 2], member(at, group - 1),
                ),
                group > 0,
            )

        @pl.when(group == 0)
        def _():
            from_previous[it] = jnp.zeros_like(from_previous[it])

        @pl.when(group == lines - 1)
        def _():
            from_following[it] = jnp.zeros_like(from_following[it])

        if it == 1:
            arrived(atoms_b.at[0, :, pl.ds(0, 3)], full_r.at[0])
            arrived(codes_b, codes_r.at[1])
            for side in range(2):
                advance(0, side)

        arrived(shares.at[it, pl.ds(0, team - 1)], halo_r.at[it, 0])
        pl.when(group > 0)(functools.partial(arrived, from_previous.at[it], halo_r.at[it, 1]))
        pl.when(group < lines - 1)(functools.partial(arrived, from_following.at[it], halo_r.at[it, 2]))
        for p in range(early, pieces) if it else ():
            share_atoms(it, p)

        total, head, tail = shares[it, 0], from_previous[it, 0], from_following[it, 0]
        for at in range(1, team):
            total, head, tail = total + shares[it, at], head + from_previous[it, at], tail + from_following[it, at]
        residual = jnp.concatenate(
            [total[:, :lag_count] + head, total[:, lag_count:width], total[:, width:] + tail], axis=1
        )
        lane = lax.broadcasted_iota(jnp.int32, residual.shape, 1)
        known = width + lag_count * jnp.minimum(lines - 1 - group, 1)
        residual = jnp.where(lane < known, residual, 0.0)
        if last:
            extended_ref[...] = residual
            residual_store = pltpu.make_async_copy(extended_ref.at[:, lanes_of(pos)], residual_out, local_sem.at[1])
            residual_store.start()
        fill_frames(frames, residual.astype(BF16).astype(F32))

        for side in range(2):
            total = None
            for i in range(width // half):
                codes = codes_main[0, :, :, pl.ds(i * half, half)].reshape(lines * rows, half)
                term = jnp.dot(codes, frames[:, pl.ds((i + side) * half, half)], preferred_element_type=F32)
                total = term if total is None else total + term
            grad[:, :, pl.ds(side * half, half)] = total.reshape(lines, rows, half)
            sum_send[it, side] = total.reshape(lines, rows, half).astype(BF16)
            for mate in mates:
                if not last:
                    start(copy_to(sum_send.at[it, side], sum_recv.at[group, side], 3, sum_r.at[0], member(pos, mate)))
                else:
                    start(
                        copy_to(sum_send.at[it, side, mate], last_recv.at[group, side], 3, sum_r.at[1], member(pos, mate))
                    )

        if not last:
            for p in range(pieces) if it == 0 else ():
                share_atoms(0, p)
            advance_main(it)
            arrived(rest.at[pl.ds(0, lines - 1)], line_r.at[1])
            for mate in mates:
                atoms_ref[mate] = atoms_b[0, mate, chip].astype(F32) + rest[mate].astype(F32)
            arrived(sum_recv.at[pl.ds(0, lines - 1)], sum_r.at[0])
            total = grad[...]
            for mate in mates:
                theirs = jnp.concatenate([sum_recv[mate, 0], sum_recv[mate, 1]], axis=2)
                total = total + theirs.astype(F32)
            updated = atoms_ref[...] + factor * total
            fresh = updated / jnp.sqrt(jnp.mean(updated * updated, axis=2, keepdims=True) + EPSILON)
            atoms_ref[...] = fresh
            atoms_b[it + 1, :, chip] = fresh.astype(BF16)
            for p in range(early):
                share_atoms(it + 1, p)
            continue

        arrived(atoms_b.at[it, :, pl.ds(0, 3)], full_r.at[it])
        advance(it, 1 - core)
        start(copy_to(codes_b.at[:, :, :, lanes_of(1 - core)], codes_out.at[:, :, core], 1, out_r.at[0], partner))
        advance(it, core)
        store = pltpu.make_async_copy(codes_b.at[:, :, :, lanes_of(core)], codes_out.at[:, :, core], local_sem.at[0])
        store.start()
        arrived(last_recv.at[pl.ds(0, lines - 1)], sum_r.at[1])
        total = grad[group]
        for mate in mates:
            total = total + jnp.concatenate([last_recv[mate, 0], last_recv[mate, 1]], axis=1).astype(F32)
        updated = atoms_ref[group] + factor * total
        atoms_ref[group] = updated / jnp.sqrt(jnp.mean(updated * updated, axis=1, keepdims=True) + EPSILON)
        atoms_store = pltpu.make_async_copy(atoms_ref.at[group], atoms_out, local_sem.at[2])
        atoms_store.start()

    arrived(codes_out.at[:, :, 1 - core], out_r.at[0])
    for put in (store, residual_store, atoms_store):
        put.wait()
    for copy, when in sent:
        if when is None:
            copy.wait_send()
        else:
            pl.when(when)(copy.wait_send)


def on_device(n, signal, codes, dictionary, thresholds):
    _, atom_count, time_len = codes.shape
    rows, lag_count = dictionary.shape
    lines, team = n // 8, 8
    width, half = team * time_len, lag_count // 2
    vmem, dma = pltpu.VMEM, pltpu.SemaphoreType.DMA
    outside = pl.BlockSpec(memory_space=pltpu.HBM)
    piece = (rows, lag_count)
    split = (lines, 4, 2, rows, time_len)
    given = [
        pltpu.with_memory_space_constraint(x, pltpu.HBM)
        for x in (signal, codes.reshape(split), dictionary, thresholds[None, :])
    ]
    made = tuple(
        pl.pallas_call(
            functools.partial(kernel, n),
            name="learn",
            out_shape=(vmem(split, BF16), vmem(piece, F32), vmem(signal.shape, F32)),
            in_specs=[outside] * 4,
            out_specs=(pl.BlockSpec(memory_space=pl.ANY),) * 3,
            scratch_shapes=[
                vmem((lines, *piece), F32),
                vmem((lines, *piece), BF16),
                vmem(signal.shape, F32),
                vmem((1, atom_count), F32),
                vmem((atom_count, 1), F32),
                vmem((lines, 4, rows, 1), F32),
                vmem((lines, 4, rows, 2 * time_len), BF16),
                vmem((lines, 4, rows, 2 * time_len), F32),
                vmem((ITERS, lines, 4, *piece), BF16),
                vmem((2, lines, rows, width + half), BF16),
                vmem((half, width + half), F32),
                vmem((half, width + half), BF16),
                vmem((lines, *piece), F32),
                vmem((1, width + lag_count), F32),
                vmem((ITERS, team, 1, width + lag_count), F32),
                vmem((ITERS, team, 1, lag_count), F32),
                vmem((ITERS, team, 1, lag_count), F32),
                vmem((ITERS, 2, lines, rows, half), BF16),
                vmem((lines, 2, lines, rows, half), BF16),
                vmem((lines, 2, rows, half), BF16),
                dma((3,)),
                dma((4,)),
                dma((2,)),
                dma((ITERS, 3)),
                dma((2,)),
                dma((2,)),
                dma((ITERS,)),
                dma((1,)),
            ],
            compiler_params=pltpu.CompilerParams(
                collective_id=0, has_side_effects=True, vmem_limit_bytes=48_000_000
            ),
        )(*given)
    )

    def publish(codes_ref, atoms_ref, residual_ref, codes_out, atoms_out, residual_out, sems):
        pairs = [(codes_ref, codes_out), (atoms_ref, atoms_out), (residual_ref, residual_out)]
        puts = [pltpu.make_async_copy(src, dst, sems.at[i]) for i, (src, dst) in enumerate(pairs)]
        for put in puts:
            put.start()
        for put in puts:
            put.wait()

    codes_out, atoms_out, residual_out = pl.pallas_call(
        publish,
        name="publish",
        out_shape=tuple(jax.ShapeDtypeStruct(x.shape, x.dtype) for x in made),
        in_specs=[pl.BlockSpec(memory_space=pl.ANY)] * 3,
        out_specs=(outside,) * 3,
        scratch_shapes=[dma((3,))],
        compiler_params=pltpu.CompilerParams(vmem_limit_bytes=1_000_000),
    )(*made)
    return codes_out.reshape(codes.shape), atoms_out, residual_out


def solution(mesh):
    return jax.shard_map(
        functools.partial(on_device, mesh.shape["tm"]),
        mesh=mesh,
        in_specs=(P("groups", "tm"), P("groups", None, "tm"), P("tm", None), P()),
        out_specs=(P("groups", None, "tm"), P(("groups", "tm"), None), P("groups", "tm")),
        check_vma=False,
    )
```

```python
import functools

import jax
import jax.numpy as jnp
from jax import lax
from jax.experimental import pallas as pl
from jax.experimental.pallas import tpu as pltpu
from jax.sharding import PartitionSpec as P

ITERS = 2
CODE_STEP = 6.0
EPSILON = 1e-06
LANES = 128
MESH = pl.DeviceIdType.MESH
BF16, F32 = jnp.bfloat16, jnp.float32
PIECES = 1


def pieces_of(rows):
    return max(1, min(PIECES, rows // 16))


def rolled(x, shift):
    width = x.shape[1]
    shift = shift % width
    return x if shift == 0 else pltpu.roll(x, shift, 1)


def lanes_from(ref, row, start, width):
    length = ref.shape[1]
    low, high = max(start, 0), min(start + width, length)
    if low >= high:
        return jnp.zeros((8, width), F32)
    pieces = [ref[pl.ds(row, 8), pl.ds(low, high - low)]]
    if low > start:
        pieces.insert(0, jnp.zeros((8, low - start), F32))
    if start + width > high:
        pieces.append(jnp.zeros((8, start + width - high), F32))
    return pieces[0] if len(pieces) == 1 else jnp.concatenate(pieces, axis=1)


def skew_total(lagged, start, length):
    total = None
    for a in range(LANES // 8):
        part = None
        for b in range(lagged.shape[0] // LANES):
            block = lanes_from(lagged, b * LANES + a * 8, start - LANES - b * LANES, length + LANES)
            part = block if part is None else part + block
        part = rolled(part, 8 * a)
        total = part if total is None else total + part
    for step in (4, 2, 1):
        total = total + pltpu.roll(rolled(total, step), 8 - step, 0)
    return total[0:1, LANES:]


def fill_frames(frames, extended, start, length):
    width = length + 2 * LANES
    base = jnp.broadcast_to(extended[:, start : start + width], (8, width))
    row = lax.broadcasted_iota(jnp.int32, (8, width), 0)
    for step in (1, 2, 4):
        base = jnp.where((row // step) % 2 == 1, rolled(base, width - step), base)
    for a in range(LANES // 16):
        low, high = rolled(base, width - 16 * a), rolled(base, width - 16 * a - 8)
        both = jnp.concatenate([low, high], axis=0).astype(BF16)
        for b in range(frames.shape[0] // LANES):
            frames[pl.ds(b * LANES + a * 16, 16), pl.ds(start, length)] = both[:, b * LANES : b * LANES + length]


def kernel(
    n, signal_hbm, codes_hbm, dictionary_hbm, thresholds_hbm,
    codes_out, atoms_out, residual_out,
    atoms_ref, rest, signal_ref, thresholds_ref, cutoffs_all, cutoffs, codes_b, current, atoms_b, codes_main, lagged,
    frames, grad, extended_ref, shares, from_previous, from_following,
    sum_send, sum_recv, last_recv,
    local_sem, send_sem, codes_r, halo_r, line_r, sum_r, full_r, out_r,
):
    rows, lag_count = dictionary_hbm.shape
    _, lines, _, length = codes_main.shape
    team = 8
    half = lag_count // 2
    width = length - half
    atom_count = lines * team * rows
    factor = (atom_count * lag_count) ** (-0.5)
    slab_len = width // 4
    pieces = pieces_of(rows)
    part = rows // pieces
    me = lax.axis_index("tm")
    pos, group = me % team, me // team
    core, chip = pos % 2, pos // 2

    def flipped(bits):
        at = 0
        for bit in (4, 2, 1):
            one = (pos // bit) % 2
            at = at + bit * ((1 - one) if bits & bit else one)
        return at

    def member(at, group_of=group):
        return group_of * team + at

    partner = member(flipped(1))
    mates = [(group + k) % lines for k in range(1, lines)]

    def copy_to(src, dst, send, recv_sem, target):
        return pltpu.make_async_remote_copy(
            src_ref=src, dst_ref=dst, send_sem=send_sem.at[send], recv_sem=recv_sem,
            device_id={"tm": target}, device_id_type=MESH,
        )

    def arrived(ref, recv_sem):
        pltpu.make_async_copy(ref, ref, recv_sem).wait()

    sent = []

    def start(copy, when=None):
        if when is None:
            copy.start()
        else:
            pl.when(when)(copy.start)
        sent.append((copy, when))

    def lanes_of(at):
        return pl.ds(pl.multiple_of(at * lag_count, LANES), lag_count)

    def slab(p):
        return pl.ds(p * part, part)

    loads = [
        pltpu.make_async_copy(dictionary_hbm, atoms_ref.at[group], local_sem.at[0]),
        pltpu.make_async_copy(signal_hbm, signal_ref, local_sem.at[1]),
        pltpu.make_async_copy(thresholds_hbm, thresholds_ref, local_sem.at[2]),
        pltpu.make_async_copy(codes_hbm.at[:, chip, core], codes_main.at[0, :, :, lanes_of(pos)], codes_r.at[0]),
        pltpu.make_async_copy(codes_hbm.at[:, :, core], codes_b.at[:, :, :, lanes_of(core)], codes_r.at[1]),
    ]
    for load in loads:
        load.start()

    barrier = pltpu.get_barrier_semaphore()

    def greet(target):
        pl.semaphore_signal(barrier, inc=1, device_id={"tm": target}, device_id_type=MESH)

    for bits in range(1, team):
        greet(member(flipped(bits)))
    for mate in mates:
        greet(member(pos, mate))

    loads[0].wait()
    atoms_b[0, group, chip] = atoms_ref[group].astype(BF16)
    rest[group] = (atoms_ref[group] - atoms_b[0, group, chip].astype(F32)).astype(BF16)
    pl.semaphore_wait(barrier, team - 1 + lines - 1)

    for mate in mates:
        held = atoms_b.at[0, group, chip]
        start(copy_to(held, held, 0, line_r.at[0], member(pos, mate)))
    for bits in (7, 6, 3, 2, 5, 4, 1):
        at = flipped(bits)
        start(
            copy_to(
                codes_hbm.at[:, at // 2, at % 2], codes_main.at[0, :, :, lanes_of(pos)], 1, codes_r.at[0], member(at)
            )
        )
    start(copy_to(codes_hbm.at[:, :, 1 - core], codes_b.at[:, :, :, lanes_of(core)], 1, codes_r.at[1], partner))
    codes_main[0, :, :, pl.ds(width, half)] = jnp.zeros((lines, rows, half), BF16)
    codes_main[1, :, :, pl.ds(0, half)] = jnp.zeros((lines, rows, half), BF16)
    loads[2].wait()
    cutoffs_all[...] = CODE_STEP * jnp.broadcast_to(thresholds_ref[...], (8, atom_count)).T[:, 0:1]
    for i in range(lines):
        for u in range(team // 2):
            at = pl.multiple_of((i * team + 2 * u + core) * rows, rows)
            cutoffs[i, u] = cutoffs_all[pl.ds(at, rows), :]
    loads[1].wait()
    extended_ref[0] = jnp.zeros((1, width + lag_count), F32)
    extended_ref[0, :, lanes_of(pos)] = signal_ref[...]

    def share_atoms(it, p):
        held = atoms_b.at[it, :, chip, slab(p), :]
        for bits in (4, 6, 2):
            start(copy_to(held, held, 0, full_r.at[it, bits // 2 - 1], member(flipped(bits))))

    def shrunk(before, matched, cutoff):
        shrink = before + (CODE_STEP * factor) * matched
        return shrink - jnp.minimum(jnp.maximum(shrink, -cutoff), cutoff)

    def product(atoms, at):
        low = jnp.dot(atoms[:, :half], frames[:, pl.ds(at, lag_count)], preferred_element_type=F32)
        return low + jnp.dot(atoms[:, half:], frames[:, pl.ds(at + half, lag_count)], preferred_element_type=F32)

    def advance(it, side, rows_of, count):
        at = pl.multiple_of((2 * chip + side) * lag_count, LANES)
        matched = product(atoms_b[(it, *rows_of)].reshape(count * rows, lag_count), at)
        store = (*rows_of, slice(None), lanes_of(side))
        before = codes_b[store].astype(F32) if it == 0 else current[store]
        after = shrunk(before, matched.reshape(count, rows, lag_count), cutoffs[rows_of])
        if it < ITERS - 1:
            current[store] = after
        codes_b[store] = after.astype(BF16)

    def wait_full(it, bits):
        arrived(atoms_b.at[it, :, flipped(bits) // 2], full_r.at[it, bits // 2 - 1])

    def advance_main(it):
        atoms = atoms_b[it, :, chip].reshape(lines * rows, lag_count)
        cutoff = cutoffs[:, chip]
        for i in range(team):
            store = (slice(None), slice(None), pl.ds(i * lag_count, lag_count))
            matched = product(atoms, i * lag_count).reshape(lines, rows, lag_count)
            if it == 0:
                before = codes_main[(0, *store)].astype(F32)
            after = shrunk(before, matched, cutoff).astype(BF16)
            codes_main[(0, *store)] = after
            codes_main[1, :, :, pl.ds(i * lag_count + half, lag_count)] = after

    early = 0
    whole, chunk = width + lag_count, 5 * half

    for it in range(ITERS):
        last = it == ITERS - 1
        if it == 0:
            arrived(atoms_b.at[0, pl.ds(0, lines - 1), 0], line_r.at[0])
            arrived(codes_main.at[0, :, :, pl.ds(0, width)], codes_r.at[0])
            for mate in mates:
                start(copy_to(rest.at[group], rest.at[group], 0, line_r.at[1], member(pos, mate)))
            codes_main[1, :, :, pl.ds(half, width)] = codes_main[0, :, :, pl.ds(0, width)]
        atoms = atoms_b[it, :, chip].reshape(lines * rows, lag_count)
        pair = jnp.concatenate([atoms[:, :half], atoms[:, half:]], axis=0)

        def correlate(at):
            picked = pl.ds(at, min(chunk, length - at))
            lagged[:, picked] = lax.dot_general(
                pair, codes_main[:, :, :, picked].reshape(2 * lines * rows, picked.size),
                (((0,), (0,)), ((), ())), preferred_element_type=F32,
            )

        correlate(0)
        for at in range(0, whole, chunk):
            if at + chunk < length:
                correlate(at + chunk)
            span = pl.ds(at, min(chunk, whole - at))
            shares[it, pos, :, span] = extended_ref[0, :, span] - factor * skew_total(lagged, at, span.size)
            if at // chunk % 2 == 0:
                continue
            held = shares.at[it, pos, :, pl.ds(at - chunk, chunk + span.size)]
            for bits in (7, 6, 3, 2, 5, 4, 1):
                start(copy_to(held, held, 2, halo_r.at[it, 0], member(flipped(bits))))
            if at == chunk:
                for to in range(team):
                    start(
                        copy_to(
                            shares.at[it, pos, :, pl.ds(0, lag_count)], from_following.at[it, pos],
                            2, halo_r.at[it, 2], member(to, group - 1),
                        ),
                        group > 0,
                    )
        for to in range(team):
            start(
                copy_to(
                    shares.at[it, pos, :, pl.ds(width, lag_count)], from_previous.at[it, pos],
                    2, halo_r.at[it, 1], member(to, group + 1),
                ),
                group < lines - 1,
            )
        for p in range(early, pieces) if it else ():
            share_atoms(it, p)

        @pl.when(group == 0)
        def _():
            from_previous[it] = jnp.zeros_like(from_previous[it])

        @pl.when(group == lines - 1)
        def _():
            from_following[it] = jnp.zeros_like(from_following[it])

        if it == 1:
            for bits in (6, 2, 4):
                wait_full(0, bits)
            arrived(codes_b, codes_r.at[1])
            for i in range(lines):
                for side in range(2):
                    advance(0, side, (i, slice(None)), team // 2)

        arrived(shares.at[it, pl.ds(0, team - 1)], halo_r.at[it, 0])
        pl.when(group > 0)(functools.partial(arrived, from_previous.at[it], halo_r.at[it, 1]))
        pl.when(group < lines - 1)(functools.partial(arrived, from_following.at[it], halo_r.at[it, 2]))
        total, head, tail = shares[it, 0], from_previous[it, 0], from_following[it, 0]
        for at in range(1, team):
            total, head, tail = total + shares[it, at], head + from_previous[it, at], tail + from_following[it, at]
        residual = jnp.concatenate(
            [total[:, :lag_count] + head, total[:, lag_count:width], total[:, width:] + tail], axis=1
        )
        lane = lax.broadcasted_iota(jnp.int32, residual.shape, 1)
        known = width + lag_count * jnp.minimum(lines - 1 - group, 1)
        residual = jnp.where(lane < known, residual, 0.0)
        if last:
            extended_ref[1] = residual
            residual_store = pltpu.make_async_copy(extended_ref.at[1, :, lanes_of(pos)], residual_out, local_sem.at[1])
            residual_store.start()
        residual = residual.astype(BF16).astype(F32)
        fill_frames(frames, residual, 0, length)

        def term(i, side):
            codes = codes_main[0, :, :, pl.ds(i * half, half)].reshape(lines * rows, half)
            return jnp.dot(codes, frames[:, pl.ds((i + side) * half, half)], preferred_element_type=F32)

        for side in range(2):
            total = None
            for i in range(width // half):
                total = term(i, side) if total is None else total + term(i, side)
            grad[:, :, pl.ds(side * half, half)] = total.reshape(lines, rows, half)
            sum_send[it, side] = total.reshape(lines, rows, half).astype(BF16)
            for mate in mates:
                if not last:
                    start(copy_to(sum_send.at[it, side], sum_recv.at[group, side], 3, sum_r.at[0], member(pos, mate)))
                else:
                    start(
                        copy_to(sum_send.at[it, side, mate], last_recv.at[group, side], 3, sum_r.at[1], member(pos, mate))
                    )

        if not last:
            for p in range(pieces) if it == 0 else ():
                share_atoms(0, p)
            advance_main(it)
            arrived(rest.at[pl.ds(0, lines - 1)], line_r.at[1])
            for mate in mates:
                atoms_ref[mate] = atoms_b[0, mate, chip].astype(F32) + rest[mate].astype(F32)
            arrived(sum_recv.at[pl.ds(0, lines - 1)], sum_r.at[0])
            total = grad[...]
            for mate in mates:
                theirs = jnp.concatenate([sum_recv[mate, 0], sum_recv[mate, 1]], axis=2)
                total = total + theirs.astype(F32)
            updated = atoms_ref[...] + factor * total
            fresh = updated / jnp.sqrt(jnp.mean(updated * updated, axis=2, keepdims=True) + EPSILON)
            atoms_ref[...] = fresh
            atoms_b[it + 1, :, chip] = fresh.astype(BF16)
            for p in range(early):
                share_atoms(it + 1, p)
            continue

        for bits in (0, 2, 4, 6):
            at = flipped(bits) // 2
            if bits:
                wait_full(it, bits)
            advance(it, 1 - core, (slice(None), at), lines)
            give = codes_b.at[:, at, :, lanes_of(1 - core)]
            start(copy_to(give, codes_out.at[:, at, core], 1, out_r.at[0], partner))
            advance(it, core, (slice(None), at), lines)
            keep = codes_b.at[:, at, :, lanes_of(core)]
            pltpu.make_async_copy(keep, codes_out.at[:, at, core], local_sem.at[0]).start()
        arrived(last_recv.at[pl.ds(0, lines - 1)], sum_r.at[1])
        total = grad[group]
        for mate in mates:
            total = total + jnp.concatenate([last_recv[mate, 0], last_recv[mate, 1]], axis=1).astype(F32)
        updated = atoms_ref[group] + factor * total
        atoms_ref[group] = updated / jnp.sqrt(jnp.mean(updated * updated, axis=1, keepdims=True) + EPSILON)
        atoms_store = pltpu.make_async_copy(atoms_ref.at[group], atoms_out, local_sem.at[2])
        atoms_store.start()

    arrived(codes_out.at[:, :, 1 - core], out_r.at[0])
    arrived(codes_out.at[:, :, core], local_sem.at[0])
    for put in (residual_store, atoms_store):
        put.wait()
    for copy, when in sent:
        if when is None:
            copy.wait_send()
        else:
            pl.when(when)(copy.wait_send)


def on_device(n, signal, codes, dictionary, thresholds):
    _, atom_count, time_len = codes.shape
    rows, lag_count = dictionary.shape
    lines, team = n // 8, 8
    width, half = team * time_len, lag_count // 2
    vmem, dma = pltpu.VMEM, pltpu.SemaphoreType.DMA
    outside = pl.BlockSpec(memory_space=pltpu.HBM)
    piece = (rows, lag_count)
    split = (lines, 4, 2, rows, time_len)
    given = [
        pltpu.with_memory_space_constraint(x, pltpu.HBM)
        for x in (signal, codes.reshape(split), dictionary, thresholds[None, :])
    ]
    made = tuple(
        pl.pallas_call(
            functools.partial(kernel, n),
            name="learn",
            out_shape=(vmem(split, BF16), vmem(piece, F32), vmem(signal.shape, F32)),
            in_specs=[outside] * 4,
            out_specs=(pl.BlockSpec(memory_space=pl.ANY),) * 3,
            scratch_shapes=[
                vmem((lines, *piece), F32),
                vmem((lines, *piece), BF16),
                vmem(signal.shape, F32),
                vmem((1, atom_count), F32),
                vmem((atom_count, 1), F32),
                vmem((lines, 4, rows, 1), F32),
                vmem((lines, 4, rows, 2 * time_len), BF16),
                vmem((lines, 4, rows, 2 * time_len), F32),
                vmem((ITERS, lines, 4, *piece), BF16),
                vmem((2, lines, rows, width + half), BF16),
                vmem((half, width + half), F32),
                vmem((half, width + half), BF16),
                vmem((lines, *piece), F32),
                vmem((2, 1, width + lag_count), F32),
                vmem((ITERS, team, 1, width + lag_count), F32),
                vmem((ITERS, team, 1, lag_count), F32),
                vmem((ITERS, team, 1, lag_count), F32),
                vmem((ITERS, 2, lines, rows, half), BF16),
                vmem((lines, 2, lines, rows, half), BF16),
                vmem((lines, 2, rows, half), BF16),
                dma((3,)),
                dma((4,)),
                dma((2,)),
                dma((ITERS, 3)),
                dma((2,)),
                dma((2,)),
                dma((ITERS, 3)),
                dma((1,)),
            ],
            compiler_params=pltpu.CompilerParams(
                collective_id=0, has_side_effects=True, vmem_limit_bytes=48_000_000
            ),
        )(*given)
    )

    def publish(codes_ref, atoms_ref, residual_ref, codes_out, atoms_out, residual_out, sems):
        pairs = [(codes_ref.at[:, i], codes_out.at[:, i]) for i in range(codes_ref.shape[1])]
        pairs += [(atoms_ref, atoms_out), (residual_ref, residual_out)]
        puts = [pltpu.make_async_copy(src, dst, sems.at[i]) for i, (src, dst) in enumerate(pairs)]
        for put in puts:
            put.start()
        for put in puts:
            put.wait()

    codes_out, atoms_out, residual_out = pl.pallas_call(
        publish,
        name="publish",
        out_shape=tuple(jax.ShapeDtypeStruct(x.shape, x.dtype) for x in made),
        in_specs=[pl.BlockSpec(memory_space=pl.ANY)] * 3,
        out_specs=(outside,) * 3,
        scratch_shapes=[dma((6,))],
        compiler_params=pltpu.CompilerParams(vmem_limit_bytes=1_000_000),
    )(*made)
    return codes_out.reshape(codes.shape), atoms_out, residual_out


def solution(mesh):
    return jax.shard_map(
        functools.partial(on_device, mesh.shape["tm"]),
        mesh=mesh,
        in_specs=(P("groups", "tm"), P("groups", None, "tm"), P("tm", None), P()),
        out_specs=(P("groups", None, "tm"), P(("groups", "tm"), None), P("groups", "tm")),
        check_vma=False,
    )
```

```python
import functools

import jax
import jax.numpy as jnp
from jax import lax
from jax.experimental import pallas as pl
from jax.experimental.pallas import tpu as pltpu
from jax.sharding import PartitionSpec as P

ITERS = 2
CODE_STEP = 6.0
EPSILON = 1e-06
LANES = 128
MESH = pl.DeviceIdType.MESH
BF16, F32 = jnp.bfloat16, jnp.float32
PIECES = 1


def pieces_of(rows):
    return max(1, min(PIECES, rows // 16))


def rolled(x, shift):
    width = x.shape[1]
    shift = shift % width
    return x if shift == 0 else pltpu.roll(x, shift, 1)


def lanes_from(ref, row, start, width):
    length = ref.shape[1]
    low, high = max(start, 0), min(start + width, length)
    if low >= high:
        return jnp.zeros((8, width), F32)
    pieces = [ref[pl.ds(row, 8), pl.ds(low, high - low)]]
    if low > start:
        pieces.insert(0, jnp.zeros((8, low - start), F32))
    if start + width > high:
        pieces.append(jnp.zeros((8, start + width - high), F32))
    return pieces[0] if len(pieces) == 1 else jnp.concatenate(pieces, axis=1)


def skew_total(lagged, start, length):
    total = None
    for a in range(LANES // 8):
        part = None
        for b in range(lagged.shape[0] // LANES):
            block = lanes_from(lagged, b * LANES + a * 8, start - LANES - b * LANES, length + LANES)
            part = block if part is None else part + block
        part = rolled(part, 8 * a)
        total = part if total is None else total + part
    for step in (4, 2, 1):
        total = total + pltpu.roll(rolled(total, step), 8 - step, 0)
    return total[0:1, LANES:]


def fill_frames(frames, extended, start, length):
    width = length + 2 * LANES
    base = jnp.broadcast_to(extended[:, start : start + width], (8, width))
    row = lax.broadcasted_iota(jnp.int32, (8, width), 0)
    for step in (1, 2, 4):
        base = jnp.where((row // step) % 2 == 1, rolled(base, width - step), base)
    for a in range(LANES // 16):
        low, high = rolled(base, width - 16 * a), rolled(base, width - 16 * a - 8)
        both = jnp.concatenate([low, high], axis=0).astype(BF16)
        for b in range(frames.shape[0] // LANES):
            frames[pl.ds(b * LANES + a * 16, 16), pl.ds(start, length)] = both[:, b * LANES : b * LANES + length]


def kernel(
    n, signal_hbm, codes_hbm, dictionary_hbm, thresholds_hbm,
    codes_out, atoms_out, residual_out,
    atoms_ref, rest, signal_ref, thresholds_ref, cutoffs_all, cutoffs, codes_b, current, atoms_b, codes_main, lagged,
    frames, grad, extended_ref, shares, from_previous, from_following,
    sum_send, sum_recv, last_recv,
    local_sem, send_sem, codes_r, halo_r, line_r, sum_r, full_r, out_r,
):
    rows, lag_count = dictionary_hbm.shape
    _, lines, _, length = codes_main.shape
    team = 8
    half = lag_count // 2
    width = length - half
    atom_count = lines * team * rows
    factor = (atom_count * lag_count) ** (-0.5)
    slab_len = width // 4
    pieces = pieces_of(rows)
    part = rows // pieces
    me = lax.axis_index("tm")
    pos, group = me % team, me // team
    core, chip = pos % 2, pos // 2

    def flipped(bits):
        at = 0
        for bit in (4, 2, 1):
            one = (pos // bit) % 2
            at = at + bit * ((1 - one) if bits & bit else one)
        return at

    def member(at, group_of=group):
        return group_of * team + at

    partner = member(flipped(1))
    mates = [(group + k) % lines for k in range(1, lines)]

    def copy_to(src, dst, send, recv_sem, target):
        return pltpu.make_async_remote_copy(
            src_ref=src, dst_ref=dst, send_sem=send_sem.at[send], recv_sem=recv_sem,
            device_id={"tm": target}, device_id_type=MESH,
        )

    def arrived(ref, recv_sem):
        pltpu.make_async_copy(ref, ref, recv_sem).wait()

    sent = []

    def start(copy, when=None):
        if when is None:
            copy.start()
        else:
            pl.when(when)(copy.start)
        sent.append((copy, when))

    def ready(copies):
        sent.extend((copy, None) for copy in copies)
        return copies

    def step(body):
        pl.when(me >= 0)(body)

    def lanes_of(at):
        return pl.ds(pl.multiple_of(at * lag_count, LANES), lag_count)

    def slab(p):
        return pl.ds(p * part, part)

    loads = [
        pltpu.make_async_copy(dictionary_hbm, atoms_ref.at[group], local_sem.at[0]),
        pltpu.make_async_copy(signal_hbm, signal_ref, local_sem.at[1]),
        pltpu.make_async_copy(thresholds_hbm, thresholds_ref, local_sem.at[2]),
        pltpu.make_async_copy(codes_hbm.at[:, chip, core], codes_main.at[0, :, :, lanes_of(pos)], codes_r.at[0]),
        pltpu.make_async_copy(codes_hbm.at[:, :, core], codes_b.at[:, :, :, lanes_of(core)], codes_r.at[1]),
    ]
    for load in loads:
        load.start()

    barrier = pltpu.get_barrier_semaphore()

    def greet(target):
        pl.semaphore_signal(barrier, inc=1, device_id={"tm": target}, device_id_type=MESH)

    for bits in range(1, team):
        greet(member(flipped(bits)))
    for mate in mates:
        greet(member(pos, mate))

    loads[0].wait()
    atoms_b[0, group, chip] = atoms_ref[group].astype(BF16)
    rest[group] = (atoms_ref[group] - atoms_b[0, group, chip].astype(F32)).astype(BF16)
    pl.semaphore_wait(barrier, team - 1 + lines - 1)

    for mate in mates:
        held = atoms_b.at[0, group, chip]
        start(copy_to(held, held, 0, line_r.at[0], member(pos, mate)))
    for bits in (7, 6, 3, 2, 5, 4, 1):
        at = flipped(bits)
        start(
            copy_to(
                codes_hbm.at[:, at // 2, at % 2], codes_main.at[0, :, :, lanes_of(pos)], 1, codes_r.at[0], member(at)
            )
        )
    start(copy_to(codes_hbm.at[:, :, 1 - core], codes_b.at[:, :, :, lanes_of(core)], 1, codes_r.at[1], partner))
    codes_main[0, :, :, pl.ds(width, half)] = jnp.zeros((lines, rows, half), BF16)
    codes_main[1, :, :, pl.ds(0, half)] = jnp.zeros((lines, rows, half), BF16)
    loads[2].wait()
    cutoffs_all[...] = CODE_STEP * jnp.broadcast_to(thresholds_ref[...], (8, atom_count)).T[:, 0:1]
    for i in range(lines):
        for u in range(team // 2):
            at = pl.multiple_of((i * team + 2 * u + core) * rows, rows)
            cutoffs[i, u] = cutoffs_all[pl.ds(at, rows), :]
    loads[1].wait()
    extended_ref[0] = jnp.zeros((1, width + lag_count), F32)
    extended_ref[0, :, lanes_of(pos)] = signal_ref[...]

    def share_atoms(it, p):
        held = atoms_b.at[it, :, chip, slab(p), :]
        for bits in (4, 6, 2):
            start(copy_to(held, held, 0, full_r.at[it, bits // 2 - 1], member(flipped(bits))))

    def shrunk(before, matched, cutoff):
        shrink = before + (CODE_STEP * factor) * matched
        return shrink - jnp.minimum(jnp.maximum(shrink, -cutoff), cutoff)

    def product(atoms, at):
        low = jnp.dot(atoms[:, :half], frames[:, pl.ds(at, lag_count)], preferred_element_type=F32)
        return low + jnp.dot(atoms[:, half:], frames[:, pl.ds(at + half, lag_count)], preferred_element_type=F32)

    def advance(it, side, rows_of, count):
        at = pl.multiple_of((2 * chip + side) * lag_count, LANES)
        matched = product(atoms_b[(it, *rows_of)].reshape(count * rows, lag_count), at)
        store = (*rows_of, slice(None), lanes_of(side))
        before = codes_b[store].astype(F32) if it == 0 else current[store]
        after = shrunk(before, matched.reshape(count, rows, lag_count), cutoffs[rows_of])
        if it < ITERS - 1:
            current[store] = after
        codes_b[store] = after.astype(BF16)

    def wait_full(it, bits):
        arrived(atoms_b.at[it, :, flipped(bits) // 2], full_r.at[it, bits // 2 - 1])

    def advance_main(it):
        atoms = atoms_b[it, :, chip].reshape(lines * rows, lag_count)
        cutoff = cutoffs[:, chip]
        for i in range(team):
            store = (slice(None), slice(None), pl.ds(i * lag_count, lag_count))
            matched = product(atoms, i * lag_count).reshape(lines, rows, lag_count)
            if it == 0:
                before = codes_main[(0, *store)].astype(F32)
            after = shrunk(before, matched, cutoff).astype(BF16)
            codes_main[(0, *store)] = after
            codes_main[1, :, :, pl.ds(i * lag_count + half, lag_count)] = after

    early = 0
    whole, chunk = width + lag_count, 5 * half

    for it in range(ITERS):
        last = it == ITERS - 1
        if it == 0:
            arrived(atoms_b.at[0, pl.ds(0, lines - 1), 0], line_r.at[0])
            arrived(codes_main.at[0, :, :, pl.ds(0, width)], codes_r.at[0])
            codes_main[1, :, :, pl.ds(half, width)] = codes_main[0, :, :, pl.ds(0, width)]
        atoms = atoms_b[it, :, chip].reshape(lines * rows, lag_count)
        pair = jnp.concatenate([atoms[:, :half], atoms[:, half:]], axis=0)

        def correlate(at):
            picked = pl.ds(at, min(chunk, length - at))
            lagged[:, picked] = lax.dot_general(
                pair, codes_main[:, :, :, picked].reshape(2 * lines * rows, picked.size),
                (((0,), (0,)), ((), ())), preferred_element_type=F32,
            )

        correlate(0)
        for at in range(0, whole, chunk):
            if at + chunk < length:
                correlate(at + chunk)
            span = pl.ds(at, min(chunk, whole - at))
            shares[it, pos, :, span] = extended_ref[0, :, span] - factor * skew_total(lagged, at, span.size)
            if at // chunk % 2 == 0:
                continue
            held = shares.at[it, pos, :, pl.ds(at - chunk, chunk + span.size)]
            for bits in (7, 6, 3, 2, 5, 4, 1):
                start(copy_to(held, held, 2, halo_r.at[it, 0], member(flipped(bits))))
            if at == chunk:
                for to in range(team):
                    start(
                        copy_to(
                            shares.at[it, pos, :, pl.ds(0, lag_count)], from_following.at[it, pos],
                            2, halo_r.at[it, 2], member(to, group - 1),
                        ),
                        group > 0,
                    )
        for to in range(team):
            start(
                copy_to(
                    shares.at[it, pos, :, pl.ds(width, lag_count)], from_previous.at[it, pos],
                    2, halo_r.at[it, 1], member(to, group + 1),
                ),
                group < lines - 1,
            )
        if it == 0:
            for mate in mates:
                start(copy_to(rest.at[group], rest.at[group], 0, line_r.at[1], member(pos, mate)))
        for p in range(early, pieces) if it else ():
            share_atoms(it, p)

        @pl.when(group == 0)
        def _():
            from_previous[it] = jnp.zeros_like(from_previous[it])

        @pl.when(group == lines - 1)
        def _():
            from_following[it] = jnp.zeros_like(from_following[it])

        if it == 1:
            for bits in (6, 2, 4):
                wait_full(0, bits)
            arrived(codes_b, codes_r.at[1])
            for i in range(lines):
                for side in range(2):
                    advance(0, side, (i, slice(None)), team // 2)

        arrived(shares.at[it, pl.ds(0, team - 1)], halo_r.at[it, 0])
        pl.when(group > 0)(functools.partial(arrived, from_previous.at[it], halo_r.at[it, 1]))
        pl.when(group < lines - 1)(functools.partial(arrived, from_following.at[it], halo_r.at[it, 2]))
        total, head, tail = shares[it, 0], from_previous[it, 0], from_following[it, 0]
        for at in range(1, team):
            total, head, tail = total + shares[it, at], head + from_previous[it, at], tail + from_following[it, at]
        residual = jnp.concatenate(
            [total[:, :lag_count] + head, total[:, lag_count:width], total[:, width:] + tail], axis=1
        )
        lane = lax.broadcasted_iota(jnp.int32, residual.shape, 1)
        known = width + lag_count * jnp.minimum(lines - 1 - group, 1)
        residual = jnp.where(lane < known, residual, 0.0)
        if last:
            extended_ref[1] = residual
            residual_store = pltpu.make_async_copy(extended_ref.at[1, :, lanes_of(pos)], residual_out, local_sem.at[1])
            residual_store.start()
        residual = residual.astype(BF16).astype(F32)
        fill_frames(frames, residual, 0, length)

        def term(i, side):
            codes = codes_main[0, :, :, pl.ds(i * half, half)].reshape(lines * rows, half)
            return jnp.dot(codes, frames[:, pl.ds((i + side) * half, half)], preferred_element_type=F32)

        for side in range(2):
            if not last:
                outgoing = ready([
                    copy_to(sum_send.at[it, side], sum_recv.at[group, side], 3, sum_r.at[0], member(pos, mate))
                    for mate in mates
                ])
            else:
                outgoing = ready([
                    copy_to(sum_send.at[it, side, mate], last_recv.at[group, side], 3, sum_r.at[1], member(pos, mate))
                    for mate in mates
                ])

            @step
            def _():
                total = None
                for i in range(width // half):
                    total = term(i, side) if total is None else total + term(i, side)
                grad[:, :, pl.ds(side * half, half)] = total.reshape(lines, rows, half)
                sum_send[it, side] = total.reshape(lines, rows, half).astype(BF16)
                for copy in outgoing:
                    copy.start()

        if not last:
            for p in range(pieces) if it == 0 else ():
                share_atoms(0, p)
            step(functools.partial(advance_main, it))
            arrived(rest.at[pl.ds(0, lines - 1)], line_r.at[1])
            for mate in mates:
                atoms_ref[mate] = atoms_b[0, mate, chip].astype(F32) + rest[mate].astype(F32)
            arrived(sum_recv.at[pl.ds(0, lines - 1)], sum_r.at[0])
            total = grad[...]
            for mate in mates:
                theirs = jnp.concatenate([sum_recv[mate, 0], sum_recv[mate, 1]], axis=2)
                total = total + theirs.astype(F32)
            updated = atoms_ref[...] + factor * total
            fresh = updated / jnp.sqrt(jnp.mean(updated * updated, axis=2, keepdims=True) + EPSILON)
            atoms_ref[...] = fresh
            atoms_b[it + 1, :, chip] = fresh.astype(BF16)
            for p in range(early):
                share_atoms(it + 1, p)
            continue

        for bits in (0, 2, 4, 6):
            at = flipped(bits) // 2
            if bits:
                wait_full(it, bits)
            gives = ready([
                copy_to(
                    codes_b.at[:, at, :, lanes_of(1 - core)], codes_out.at[:, at, core], 1, out_r.at[0], partner
                )
            ])

            @step
            def _():
                advance(it, 1 - core, (slice(None), at), lines)
                gives[0].start()

            @step
            def _():
                advance(it, core, (slice(None), at), lines)
                held = codes_b.at[:, at, :, lanes_of(core)]
                pltpu.make_async_copy(held, codes_out.at[:, at, core], local_sem.at[0]).start()

        arrived(last_recv.at[pl.ds(0, lines - 1)], sum_r.at[1])
        total = grad[group]
        for mate in mates:
            total = total + jnp.concatenate([last_recv[mate, 0], last_recv[mate, 1]], axis=1).astype(F32)
        updated = atoms_ref[group] + factor * total
        atoms_out[...] = updated / jnp.sqrt(jnp.mean(updated * updated, axis=1, keepdims=True) + EPSILON)

    arrived(codes_out.at[:, :, 1 - core], out_r.at[0])
    arrived(codes_out.at[:, :, core], local_sem.at[0])
    residual_store.wait()
    for copy, when in sent:
        if when is None:
            copy.wait_send()
        else:
            pl.when(when)(copy.wait_send)


def on_device(n, signal, codes, dictionary, thresholds):
    _, atom_count, time_len = codes.shape
    rows, lag_count = dictionary.shape
    lines, team = n // 8, 8
    width, half = team * time_len, lag_count // 2
    vmem, dma = pltpu.VMEM, pltpu.SemaphoreType.DMA
    outside = pl.BlockSpec(memory_space=pltpu.HBM)
    piece = (rows, lag_count)
    split = (lines, 4, 2, rows, time_len)
    given = [
        pltpu.with_memory_space_constraint(x, pltpu.HBM)
        for x in (signal, codes.reshape(split), dictionary, thresholds[None, :])
    ]
    made = tuple(
        pl.pallas_call(
            functools.partial(kernel, n),
            name="learn",
            out_shape=(vmem(split, BF16), vmem(piece, F32), vmem(signal.shape, F32)),
            in_specs=[outside] * 4,
            out_specs=[pl.BlockSpec(memory_space=space) for space in (pl.ANY, pltpu.VMEM, pl.ANY)],
            scratch_shapes=[
                vmem((lines, *piece), F32),
                vmem((lines, *piece), BF16),
                vmem(signal.shape, F32),
                vmem((1, atom_count), F32),
                vmem((atom_count, 1), F32),
                vmem((lines, 4, rows, 1), F32),
                vmem((lines, 4, rows, 2 * time_len), BF16),
                vmem((lines, 4, rows, 2 * time_len), F32),
                vmem((ITERS, lines, 4, *piece), BF16),
                vmem((2, lines, rows, width + half), BF16),
                vmem((half, width + half), F32),
                vmem((half, width + half), BF16),
                vmem((lines, *piece), F32),
                vmem((2, 1, width + lag_count), F32),
                vmem((ITERS, team, 1, width + lag_count), F32),
                vmem((ITERS, team, 1, lag_count), F32),
                vmem((ITERS, team, 1, lag_count), F32),
                vmem((ITERS, 2, lines, rows, half), BF16),
                vmem((lines, 2, lines, rows, half), BF16),
                vmem((lines, 2, rows, half), BF16),
                dma((3,)),
                dma((4,)),
                dma((2,)),
                dma((ITERS, 3)),
                dma((2,)),
                dma((2,)),
                dma((ITERS, 3)),
                dma((1,)),
            ],
            compiler_params=pltpu.CompilerParams(
                collective_id=0, has_side_effects=True, vmem_limit_bytes=48_000_000
            ),
        )(*given)
    )

    def publish(codes_ref, atoms_ref, residual_ref, codes_out, atoms_out, residual_out, sems):
        pairs = [(codes_ref.at[:, i], codes_out.at[:, i]) for i in range(codes_ref.shape[1])]
        pairs += [(atoms_ref, atoms_out), (residual_ref, residual_out)]
        puts = [pltpu.make_async_copy(src, dst, sems.at[i]) for i, (src, dst) in enumerate(pairs)]
        for put in puts:
            put.start()
        for put in puts:
            put.wait()

    codes_out, atoms_out, residual_out = pl.pallas_call(
        publish,
        name="publish",
        out_shape=tuple(jax.ShapeDtypeStruct(x.shape, x.dtype) for x in made),
        in_specs=[pl.BlockSpec(memory_space=pl.ANY)] * 3,
        out_specs=(outside,) * 3,
        scratch_shapes=[dma((6,))],
        compiler_params=pltpu.CompilerParams(vmem_limit_bytes=1_000_000),
    )(*made)
    return codes_out.reshape(codes.shape), atoms_out, residual_out


def solution(mesh):
    return jax.shard_map(
        functools.partial(on_device, mesh.shape["tm"]),
        mesh=mesh,
        in_specs=(P("groups", "tm"), P("groups", None, "tm"), P("tm", None), P()),
        out_specs=(P("groups", None, "tm"), P(("groups", "tm"), None), P("groups", "tm")),
        check_vma=False,
    )
```

```python
import functools

import jax
import jax.numpy as jnp
from jax import lax
from jax.experimental import pallas as pl
from jax.experimental.pallas import tpu as pltpu
from jax.sharding import PartitionSpec as P

ITERS = 2
CODE_STEP = 6.0
EPSILON = 1e-06
LANES = 128
MESH = pl.DeviceIdType.MESH
BF16, F32 = jnp.bfloat16, jnp.float32
PIECES = 1


def pieces_of(rows):
    return max(1, min(PIECES, rows // 16))


def rolled(x, shift):
    width = x.shape[1]
    shift = shift % width
    return x if shift == 0 else pltpu.roll(x, shift, 1)


def lanes_from(ref, row, start, width):
    length = ref.shape[1]
    low, high = max(start, 0), min(start + width, length)
    if low >= high:
        return jnp.zeros((8, width), F32)
    pieces = [ref[pl.ds(row, 8), pl.ds(low, high - low)]]
    if low > start:
        pieces.insert(0, jnp.zeros((8, low - start), F32))
    if start + width > high:
        pieces.append(jnp.zeros((8, start + width - high), F32))
    return pieces[0] if len(pieces) == 1 else jnp.concatenate(pieces, axis=1)


def skew_total(lagged, start, length):
    total = None
    for a in range(LANES // 8):
        part = None
        for b in range(lagged.shape[0] // LANES):
            block = lanes_from(lagged, b * LANES + a * 8, start - LANES - b * LANES, length + LANES)
            part = block if part is None else part + block
        part = rolled(part, 8 * a)
        total = part if total is None else total + part
    for step in (4, 2, 1):
        total = total + pltpu.roll(rolled(total, step), 8 - step, 0)
    return total[0:1, LANES:]


def fill_frames(frames, extended, start, length):
    width = length + 2 * LANES
    base = jnp.broadcast_to(extended[:, start : start + width], (8, width))
    row = lax.broadcasted_iota(jnp.int32, (8, width), 0)
    for step in (1, 2, 4):
        base = jnp.where((row // step) % 2 == 1, rolled(base, width - step), base)
    for a in range(LANES // 16):
        low, high = rolled(base, width - 16 * a), rolled(base, width - 16 * a - 8)
        both = jnp.concatenate([low, high], axis=0).astype(BF16)
        for b in range(frames.shape[0] // LANES):
            frames[pl.ds(b * LANES + a * 16, 16), pl.ds(start, length)] = both[:, b * LANES : b * LANES + length]


def kernel(
    n, signal_hbm, codes_hbm, dictionary_hbm, thresholds_hbm,
    codes_out, atoms_out, residual_out,
    atoms_ref, rest, signal_ref, thresholds_ref, cutoffs_all, cutoffs, codes_b, current, atoms_b, codes_main, lagged,
    frames, grad, extended_ref, shares, from_previous, from_following,
    sum_send, sum_recv, last_recv,
    local_sem, send_sem, codes_r, halo_r, line_r, sum_r, full_r, out_r,
):
    rows, lag_count = dictionary_hbm.shape
    _, lines, _, length = codes_main.shape
    team = 8
    half = lag_count // 2
    width = length - half
    atom_count = lines * team * rows
    factor = (atom_count * lag_count) ** (-0.5)
    slab_len = width // 4
    pieces = pieces_of(rows)
    part = rows // pieces
    me = lax.axis_index("tm")
    pos, group = me % team, me // team
    core, chip = pos % 2, pos // 2

    def flipped(bits):
        at = 0
        for bit in (4, 2, 1):
            one = (pos // bit) % 2
            at = at + bit * ((1 - one) if bits & bit else one)
        return at

    def member(at, group_of=group):
        return group_of * team + at

    partner = member(flipped(1))
    mates = [(group + k) % lines for k in range(1, lines)]

    def copy_to(src, dst, send, recv_sem, target):
        return pltpu.make_async_remote_copy(
            src_ref=src, dst_ref=dst, send_sem=send_sem.at[send], recv_sem=recv_sem,
            device_id={"tm": target}, device_id_type=MESH,
        )

    def arrived(ref, recv_sem):
        pltpu.make_async_copy(ref, ref, recv_sem).wait()

    sent = []

    def start(copy, when=None):
        if when is None:
            copy.start()
        else:
            pl.when(when)(copy.start)
        sent.append((copy, when))

    def ready(copies):
        sent.extend((copy, None) for copy in copies)
        return copies

    def step(body):
        pl.when(me >= 0)(body)

    def lanes_of(at):
        return pl.ds(pl.multiple_of(at * lag_count, LANES), lag_count)

    def slab(p):
        return pl.ds(p * part, part)

    loads = [
        pltpu.make_async_copy(dictionary_hbm, atoms_ref.at[group], local_sem.at[0]),
        pltpu.make_async_copy(signal_hbm, signal_ref, local_sem.at[1]),
        pltpu.make_async_copy(thresholds_hbm, thresholds_ref, local_sem.at[2]),
        pltpu.make_async_copy(codes_hbm.at[:, chip, core], codes_main.at[0, :, :, lanes_of(pos)], codes_r.at[0]),
        pltpu.make_async_copy(codes_hbm.at[:, :, core], codes_b.at[:, :, :, lanes_of(core)], codes_r.at[1]),
    ]
    for load in loads:
        load.start()

    barrier = pltpu.get_barrier_semaphore()

    def greet(target):
        pl.semaphore_signal(barrier, inc=1, device_id={"tm": target}, device_id_type=MESH)

    for bits in range(1, team):
        greet(member(flipped(bits)))
    for mate in mates:
        greet(member(pos, mate))

    loads[0].wait()
    atoms_b[0, group, chip] = atoms_ref[group].astype(BF16)
    rest[group] = (atoms_ref[group] - atoms_b[0, group, chip].astype(F32)).astype(BF16)
    pl.semaphore_wait(barrier, team - 1 + lines - 1)

    for mate in mates:
        held = atoms_b.at[0, group, chip]
        start(copy_to(held, held, 0, line_r.at[0], member(pos, mate)))
    for bits in (7, 6, 5, 3, 4, 2, 1):
        at = flipped(bits)
        start(
            copy_to(
                codes_hbm.at[:, at // 2, at % 2], codes_main.at[0, :, :, lanes_of(pos)], 1, codes_r.at[0], member(at)
            )
        )
    start(copy_to(codes_hbm.at[:, :, 1 - core], codes_b.at[:, :, :, lanes_of(core)], 1, codes_r.at[1], partner))
    codes_main[0, :, :, pl.ds(width, half)] = jnp.zeros((lines, rows, half), BF16)
    codes_main[1, :, :, pl.ds(0, half)] = jnp.zeros((lines, rows, half), BF16)
    loads[2].wait()
    cutoffs_all[...] = CODE_STEP * jnp.broadcast_to(thresholds_ref[...], (8, atom_count)).T[:, 0:1]
    for i in range(lines):
        for u in range(team // 2):
            at = pl.multiple_of((i * team + 2 * u + core) * rows, rows)
            cutoffs[i, u] = cutoffs_all[pl.ds(at, rows), :]
    loads[1].wait()
    extended_ref[0] = jnp.zeros((1, width + lag_count), F32)
    extended_ref[0, :, lanes_of(pos)] = signal_ref[...]

    def share_atoms(it, p):
        held = atoms_b.at[it, :, chip, slab(p), :]
        for bits in (4, 6, 2):
            start(copy_to(held, held, 0, full_r.at[it, bits // 2 - 1], member(flipped(bits))))

    def shrunk(before, matched, cutoff):
        shrink = before + (CODE_STEP * factor) * matched
        return shrink - jnp.minimum(jnp.maximum(shrink, -cutoff), cutoff)

    def product(atoms, at):
        low = jnp.dot(atoms[:, :half], frames[:, pl.ds(at, lag_count)], preferred_element_type=F32)
        return low + jnp.dot(atoms[:, half:], frames[:, pl.ds(at + half, lag_count)], preferred_element_type=F32)

    def advance(it, side, rows_of, count):
        at = pl.multiple_of((2 * chip + side) * lag_count, LANES)
        matched = product(atoms_b[(it, *rows_of)].reshape(count * rows, lag_count), at)
        store = (*rows_of, slice(None), lanes_of(side))
        before = codes_b[store].astype(F32) if it == 0 else current[store]
        after = shrunk(before, matched.reshape(count, rows, lag_count), cutoffs[rows_of])
        if it < ITERS - 1:
            current[store] = after
        codes_b[store] = after.astype(BF16)

    def wait_full(it, bits):
        arrived(atoms_b.at[it, :, flipped(bits) // 2], full_r.at[it, bits // 2 - 1])

    def advance_main(it):
        atoms = atoms_b[it, :, chip].reshape(lines * rows, lag_count)
        cutoff = cutoffs[:, chip]
        for i in range(team):
            store = (slice(None), slice(None), pl.ds(i * lag_count, lag_count))
            matched = product(atoms, i * lag_count).reshape(lines, rows, lag_count)
            if it == 0:
                before = codes_main[(0, *store)].astype(F32)
            after = shrunk(before, matched, cutoff).astype(BF16)
            codes_main[(0, *store)] = after
            codes_main[1, :, :, pl.ds(i * lag_count + half, lag_count)] = after

    early = 0
    whole, chunk = width + lag_count, 5 * half

    for it in range(ITERS):
        last = it == ITERS - 1
        if it == 0:
            arrived(atoms_b.at[0, pl.ds(0, lines - 1), 0], line_r.at[0])
            arrived(codes_main.at[0, :, :, pl.ds(0, width)], codes_r.at[0])
            codes_main[1, :, :, pl.ds(half, width)] = codes_main[0, :, :, pl.ds(0, width)]
        atoms = atoms_b[it, :, chip].reshape(lines * rows, lag_count)
        pair = jnp.concatenate([atoms[:, :half], atoms[:, half:]], axis=0).astype(F32).T.astype(BF16)

        def correlate(at):
            picked = pl.ds(at, min(chunk, length - at))
            lagged[:, picked] = lax.dot_general(
                pair, codes_main[:, :, :, picked].reshape(2 * lines * rows, picked.size),
                (((1,), (0,)), ((), ())), preferred_element_type=F32,
            )

        correlate(0)
        for at in range(0, whole, chunk):
            if at + chunk < length:
                correlate(at + chunk)
            span = pl.ds(at, min(chunk, whole - at))
            shares[it, pos, :, span] = extended_ref[0, :, span] - factor * skew_total(lagged, at, span.size)
            if at // chunk % 2 == 0:
                continue
            held = shares.at[it, pos, :, pl.ds(at - chunk, chunk + span.size)]
            for bits in (7, 6, 5, 3, 4, 2, 1):
                start(copy_to(held, held, 2, halo_r.at[it, 0], member(flipped(bits))))
            if at == chunk:
                for to in range(team):
                    start(
                        copy_to(
                            shares.at[it, pos, :, pl.ds(0, lag_count)], from_following.at[it, pos],
                            2, halo_r.at[it, 2], member(to, group - 1),
                        ),
                        group > 0,
                    )
        for to in range(team):
            start(
                copy_to(
                    shares.at[it, pos, :, pl.ds(width, lag_count)], from_previous.at[it, pos],
                    2, halo_r.at[it, 1], member(to, group + 1),
                ),
                group < lines - 1,
            )
        if it == 0:
            for mate in mates:
                start(copy_to(rest.at[group], rest.at[group], 0, line_r.at[1], member(pos, mate)))
        for p in range(early, pieces) if it else ():
            share_atoms(it, p)

        @pl.when(group == 0)
        def _():
            from_previous[it] = jnp.zeros_like(from_previous[it])

        @pl.when(group == lines - 1)
        def _():
            from_following[it] = jnp.zeros_like(from_following[it])

        if it == 1:
            for bits in (6, 2, 4):
                wait_full(0, bits)
            arrived(codes_b, codes_r.at[1])
            for i in range(lines):
                for side in range(2):
                    advance(0, side, (i, slice(None)), team // 2)

        arrived(shares.at[it, pl.ds(0, team - 1)], halo_r.at[it, 0])
        pl.when(group > 0)(functools.partial(arrived, from_previous.at[it], halo_r.at[it, 1]))
        pl.when(group < lines - 1)(functools.partial(arrived, from_following.at[it], halo_r.at[it, 2]))
        total, head, tail = shares[it, 0], from_previous[it, 0], from_following[it, 0]
        for at in range(1, team):
            total, head, tail = total + shares[it, at], head + from_previous[it, at], tail + from_following[it, at]
        residual = jnp.concatenate(
            [total[:, :lag_count] + head, total[:, lag_count:width], total[:, width:] + tail], axis=1
        )
        lane = lax.broadcasted_iota(jnp.int32, residual.shape, 1)
        known = width + lag_count * jnp.minimum(lines - 1 - group, 1)
        residual = jnp.where(lane < known, residual, 0.0)
        if last:
            extended_ref[1] = residual
            residual_store = pltpu.make_async_copy(extended_ref.at[1, :, lanes_of(pos)], residual_out, local_sem.at[1])
            residual_store.start()
        residual = residual.astype(BF16).astype(F32)
        fill_frames(frames, residual, 0, length)

        def term(i, side):
            codes = codes_main[0, :, :, pl.ds(i * half, half)].reshape(lines * rows, half)
            return jnp.dot(codes, frames[:, pl.ds((i + side) * half, half)], preferred_element_type=F32)

        for side in range(2):
            if not last:
                outgoing = ready([
                    copy_to(sum_send.at[it, side], sum_recv.at[group, side], 3, sum_r.at[0], member(pos, mate))
                    for mate in mates
                ])
            else:
                outgoing = ready([
                    copy_to(sum_send.at[it, side, mate], last_recv.at[group, side], 3, sum_r.at[1], member(pos, mate))
                    for mate in mates
                ])

            @step
            def _():
                total = None
                for i in range(width // half):
                    total = term(i, side) if total is None else total + term(i, side)
                grad[:, :, pl.ds(side * half, half)] = total.reshape(lines, rows, half)
                sum_send[it, side] = total.reshape(lines, rows, half).astype(BF16)
                for copy in outgoing:
                    copy.start()

        if not last:
            for p in range(pieces) if it == 0 else ():
                share_atoms(0, p)
            step(functools.partial(advance_main, it))
            arrived(rest.at[pl.ds(0, lines - 1)], line_r.at[1])
            for mate in mates:
                atoms_ref[mate] = atoms_b[0, mate, chip].astype(F32) + rest[mate].astype(F32)
            arrived(sum_recv.at[pl.ds(0, lines - 1)], sum_r.at[0])
            total = grad[...]
            for mate in mates:
                theirs = jnp.concatenate([sum_recv[mate, 0], sum_recv[mate, 1]], axis=2)
                total = total + theirs.astype(F32)
            updated = atoms_ref[...] + factor * total
            fresh = updated / jnp.sqrt(jnp.mean(updated * updated, axis=2, keepdims=True) + EPSILON)
            atoms_ref[...] = fresh
            atoms_b[it + 1, :, chip] = fresh.astype(BF16)
            for p in range(early):
                share_atoms(it + 1, p)
            continue

        for bits in (0, 2, 4, 6):
            at = flipped(bits) // 2
            if bits:
                wait_full(it, bits)
            gives = ready([
                copy_to(
                    codes_b.at[:, at, :, lanes_of(1 - core)], codes_out.at[:, at, core], 1, out_r.at[0], partner
                )
            ])

            @step
            def _():
                advance(it, 1 - core, (slice(None), at), lines)
                gives[0].start()

            @step
            def _():
                advance(it, core, (slice(None), at), lines)
                held = codes_b.at[:, at, :, lanes_of(core)]
                pltpu.make_async_copy(held, codes_out.at[:, at, core], local_sem.at[0]).start()

        arrived(last_recv.at[pl.ds(0, lines - 1)], sum_r.at[1])
        total = grad[group]
        for mate in mates:
            total = total + jnp.concatenate([last_recv[mate, 0], last_recv[mate, 1]], axis=1).astype(F32)
        updated = atoms_ref[group] + factor * total
        atoms_out[...] = updated / jnp.sqrt(jnp.mean(updated * updated, axis=1, keepdims=True) + EPSILON)

    arrived(codes_out.at[:, :, 1 - core], out_r.at[0])
    arrived(codes_out.at[:, :, core], local_sem.at[0])
    residual_store.wait()
    for copy, when in sent:
        if when is None:
            copy.wait_send()
        else:
            pl.when(when)(copy.wait_send)


def on_device(n, signal, codes, dictionary, thresholds):
    _, atom_count, time_len = codes.shape
    rows, lag_count = dictionary.shape
    lines, team = n // 8, 8
    width, half = team * time_len, lag_count // 2
    vmem, dma = pltpu.VMEM, pltpu.SemaphoreType.DMA
    outside = pl.BlockSpec(memory_space=pltpu.HBM)
    piece = (rows, lag_count)
    split = (lines, 4, 2, rows, time_len)
    given = [
        pltpu.with_memory_space_constraint(x, pltpu.HBM)
        for x in (signal, codes.reshape(split), dictionary, thresholds[None, :])
    ]
    made = tuple(
        pl.pallas_call(
            functools.partial(kernel, n),
            name="learn",
            out_shape=(vmem(split, BF16), vmem(piece, F32), vmem(signal.shape, F32)),
            in_specs=[outside] * 4,
            out_specs=[pl.BlockSpec(memory_space=space) for space in (pl.ANY, pltpu.VMEM, pl.ANY)],
            scratch_shapes=[
                vmem((lines, *piece), F32),
                vmem((lines, *piece), BF16),
                vmem(signal.shape, F32),
                vmem((1, atom_count), F32),
                vmem((atom_count, 1), F32),
                vmem((lines, 4, rows, 1), F32),
                vmem((lines, 4, rows, 2 * time_len), BF16),
                vmem((lines, 4, rows, 2 * time_len), F32),
                vmem((ITERS, lines, 4, *piece), BF16),
                vmem((2, lines, rows, width + half), BF16),
                vmem((half, width + half), F32),
                vmem((half, width + half), BF16),
                vmem((lines, *piece), F32),
                vmem((2, 1, width + lag_count), F32),
                vmem((ITERS, team, 1, width + lag_count), F32),
                vmem((ITERS, team, 1, lag_count), F32),
                vmem((ITERS, team, 1, lag_count), F32),
                vmem((ITERS, 2, lines, rows, half), BF16),
                vmem((lines, 2, lines, rows, half), BF16),
                vmem((lines, 2, rows, half), BF16),
                dma((3,)),
                dma((4,)),
                dma((2,)),
                dma((ITERS, 3)),
                dma((2,)),
                dma((2,)),
                dma((ITERS, 3)),
                dma((1,)),
            ],
            compiler_params=pltpu.CompilerParams(
                collective_id=0, has_side_effects=True, vmem_limit_bytes=48_000_000
            ),
        )(*given)
    )

    def publish(codes_ref, atoms_ref, residual_ref, codes_out, atoms_out, residual_out, sems):
        pairs = [(codes_ref.at[:, i], codes_out.at[:, i]) for i in range(codes_ref.shape[1])]
        pairs += [(atoms_ref, atoms_out), (residual_ref, residual_out)]
        puts = [pltpu.make_async_copy(src, dst, sems.at[i]) for i, (src, dst) in enumerate(pairs)]
        for put in puts:
            put.start()
        for put in puts:
            put.wait()

    codes_out, atoms_out, residual_out = pl.pallas_call(
        publish,
        name="publish",
        out_shape=tuple(jax.ShapeDtypeStruct(x.shape, x.dtype) for x in made),
        in_specs=[pl.BlockSpec(memory_space=pl.ANY)] * 3,
        out_specs=(outside,) * 3,
        scratch_shapes=[dma((6,))],
        compiler_params=pltpu.CompilerParams(vmem_limit_bytes=1_000_000),
    )(*made)
    return codes_out.reshape(codes.shape), atoms_out, residual_out


def solution(mesh):
    return jax.shard_map(
        functools.partial(on_device, mesh.shape["tm"]),
        mesh=mesh,
        in_specs=(P("groups", "tm"), P("groups", None, "tm"), P("tm", None), P()),
        out_specs=(P("groups", None, "tm"), P(("groups", "tm"), None), P("groups", "tm")),
        check_vma=False,
    )
```

```python
import functools

import jax
import jax.numpy as jnp
from jax import lax
from jax.experimental import pallas as pl
from jax.experimental.pallas import tpu as pltpu
from jax.sharding import PartitionSpec as P

ITERS = 2
CODE_STEP = 6.0
EPSILON = 1e-06
LANES = 128
MESH = pl.DeviceIdType.MESH
BF16, F32 = jnp.bfloat16, jnp.float32
PIECES = 1


def pieces_of(rows):
    return max(1, min(PIECES, rows // 16))


def rolled(x, shift):
    width = x.shape[1]
    shift = shift % width
    return x if shift == 0 else pltpu.roll(x, shift, 1)


def lanes_from(ref, row, start, width):
    length = ref.shape[1]
    low, high = max(start, 0), min(start + width, length)
    if low >= high:
        return jnp.zeros((8, width), F32)
    pieces = [ref[pl.ds(row, 8), pl.ds(low, high - low)]]
    if low > start:
        pieces.insert(0, jnp.zeros((8, low - start), F32))
    if start + width > high:
        pieces.append(jnp.zeros((8, start + width - high), F32))
    return pieces[0] if len(pieces) == 1 else jnp.concatenate(pieces, axis=1)


def skew_total(lagged, start, length):
    total = None
    for a in range(LANES // 8):
        part = None
        for b in range(lagged.shape[0] // LANES):
            block = lanes_from(lagged, b * LANES + a * 8, start - LANES - b * LANES, length + LANES)
            part = block if part is None else part + block
        part = rolled(part, 8 * a)
        total = part if total is None else total + part
    for step in (4, 2, 1):
        total = total + pltpu.roll(rolled(total, step), 8 - step, 0)
    return total[0:1, LANES:]


def fill_frames(frames, extended, start, length):
    width = length + 2 * LANES
    base = jnp.broadcast_to(extended[:, start : start + width], (8, width))
    row = lax.broadcasted_iota(jnp.int32, (8, width), 0)
    for step in (1, 2, 4):
        base = jnp.where((row // step) % 2 == 1, rolled(base, width - step), base)
    for a in range(LANES // 16):
        low, high = rolled(base, width - 16 * a), rolled(base, width - 16 * a - 8)
        both = jnp.concatenate([low, high], axis=0).astype(BF16)
        for b in range(frames.shape[0] // LANES):
            frames[pl.ds(b * LANES + a * 16, 16), pl.ds(start, length)] = both[:, b * LANES : b * LANES + length]


def kernel(
    n, signal_hbm, codes_hbm, dictionary_hbm, thresholds_hbm,
    codes_out, atoms_out, residual_out,
    atoms_ref, rest, signal_ref, thresholds_ref, cutoffs_all, cutoffs, codes_b, current, atoms_b, codes_main, lagged,
    frames, grad, extended_ref, shares, from_previous, from_following,
    sum_send, sum_recv, last_recv,
    local_sem, send_sem, codes_r, halo_r, line_r, sum_r, full_r, out_r,
):
    rows, lag_count = dictionary_hbm.shape
    _, lines, _, length = codes_main.shape
    team = 8
    half = lag_count // 2
    width = length - half
    atom_count = lines * team * rows
    factor = (atom_count * lag_count) ** (-0.5)
    slab_len = width // 4
    pieces = pieces_of(rows)
    part = rows // pieces
    me = lax.axis_index("tm")
    pos, group = me % team, me // team
    core, chip = pos % 2, pos // 2

    def flipped(bits):
        at = 0
        for bit in (4, 2, 1):
            one = (pos // bit) % 2
            at = at + bit * ((1 - one) if bits & bit else one)
        return at

    def member(at, group_of=group):
        return group_of * team + at

    partner = member(flipped(1))
    mates = [(group + k) % lines for k in range(1, lines)]

    def copy_to(src, dst, send, recv_sem, target):
        return pltpu.make_async_remote_copy(
            src_ref=src, dst_ref=dst, send_sem=send_sem.at[send], recv_sem=recv_sem,
            device_id={"tm": target}, device_id_type=MESH,
        )

    def arrived(ref, recv_sem):
        pltpu.make_async_copy(ref, ref, recv_sem).wait()

    sent = []

    def start(copy, when=None):
        if when is None:
            copy.start()
        else:
            pl.when(when)(copy.start)
        sent.append((copy, when))

    def ready(copies):
        sent.extend((copy, None) for copy in copies)
        return copies

    def step(body):
        pl.when(me >= 0)(body)

    def lanes_of(at):
        return pl.ds(pl.multiple_of(at * lag_count, LANES), lag_count)

    def slab(p):
        return pl.ds(p * part, part)

    loads = [
        pltpu.make_async_copy(dictionary_hbm, atoms_ref.at[group], local_sem.at[0]),
        pltpu.make_async_copy(signal_hbm, signal_ref, local_sem.at[1]),
        pltpu.make_async_copy(thresholds_hbm, thresholds_ref, local_sem.at[2]),
        pltpu.make_async_copy(codes_hbm.at[:, chip, core], codes_main.at[0, :, :, lanes_of(pos)], codes_r.at[0]),
        pltpu.make_async_copy(codes_hbm.at[:, :, core], codes_b.at[:, :, :, lanes_of(core)], codes_r.at[1]),
    ]
    for load in loads:
        load.start()

    barrier = pltpu.get_barrier_semaphore()

    def greet(target):
        pl.semaphore_signal(barrier, inc=1, device_id={"tm": target}, device_id_type=MESH)

    for bits in range(1, team):
        greet(member(flipped(bits)))
    for mate in mates:
        greet(member(pos, mate))

    pl.semaphore_wait(barrier, team - 1 + lines - 1)

    def hand_over(bits):
        at = flipped(bits)
        source = codes_hbm.at[:, at // 2, at % 2]
        start(copy_to(source, codes_main.at[0, :, :, lanes_of(pos)], 1, codes_r.at[0], member(at)))

    for bits in (3, 2):
        hand_over(bits)
    loads[0].wait()
    atoms_b[0, group, chip] = atoms_ref[group].astype(BF16)
    for mate in mates:
        held = atoms_b.at[0, group, chip]
        start(copy_to(held, held, 0, line_r.at[0], member(pos, mate)))
    for bits in (7, 6, 5, 4, 1):
        hand_over(bits)
    rest[group] = (atoms_ref[group] - atoms_b[0, group, chip].astype(F32)).astype(BF16)
    start(copy_to(codes_hbm.at[:, :, 1 - core], codes_b.at[:, :, :, lanes_of(core)], 1, codes_r.at[1], partner))

    codes_main[0, :, :, pl.ds(width, half)] = jnp.zeros((lines, rows, half), BF16)
    codes_main[1, :, :, pl.ds(0, half)] = jnp.zeros((lines, rows, half), BF16)
    loads[2].wait()
    cutoffs_all[...] = CODE_STEP * jnp.broadcast_to(thresholds_ref[...], (8, atom_count)).T[:, 0:1]
    for i in range(lines):
        for u in range(team // 2):
            at = pl.multiple_of((i * team + 2 * u + core) * rows, rows)
            cutoffs[i, u] = cutoffs_all[pl.ds(at, rows), :]
    loads[1].wait()
    extended_ref[0] = jnp.zeros((1, width + lag_count), F32)
    extended_ref[0, :, lanes_of(pos)] = signal_ref[...]

    def share_atoms(it, p):
        held = atoms_b.at[it, :, chip, slab(p), :]
        for bits in (4, 6, 2):
            start(copy_to(held, held, 0, full_r.at[it, bits // 2 - 1], member(flipped(bits))))

    def shrunk(before, matched, cutoff):
        shrink = before + (CODE_STEP * factor) * matched
        return shrink - jnp.minimum(jnp.maximum(shrink, -cutoff), cutoff)

    def product(atoms, at):
        low = jnp.dot(atoms[:, :half], frames[:, pl.ds(at, lag_count)], preferred_element_type=F32)
        return low + jnp.dot(atoms[:, half:], frames[:, pl.ds(at + half, lag_count)], preferred_element_type=F32)

    def advance(it, side, rows_of, count):
        at = pl.multiple_of((2 * chip + side) * lag_count, LANES)
        matched = product(atoms_b[(it, *rows_of)].reshape(count * rows, lag_count), at)
        store = (*rows_of, slice(None), lanes_of(side))
        before = codes_b[store].astype(F32) if it == 0 else current[store]
        after = shrunk(before, matched.reshape(count, rows, lag_count), cutoffs[rows_of])
        if it < ITERS - 1:
            current[store] = after
        codes_b[store] = after.astype(BF16)

    def wait_full(it, bits):
        arrived(atoms_b.at[it, :, flipped(bits) // 2], full_r.at[it, bits // 2 - 1])

    def advance_main(it):
        atoms = atoms_b[it, :, chip].reshape(lines * rows, lag_count)
        cutoff = cutoffs[:, chip]
        for i in range(team):
            store = (slice(None), slice(None), pl.ds(i * lag_count, lag_count))
            matched = product(atoms, i * lag_count).reshape(lines, rows, lag_count)
            if it == 0:
                before = codes_main[(0, *store)].astype(F32)
            after = shrunk(before, matched, cutoff).astype(BF16)
            codes_main[(0, *store)] = after
            codes_main[1, :, :, pl.ds(i * lag_count + half, lag_count)] = after

    early = 0
    whole, chunk = width + lag_count, 5 * half

    for it in range(ITERS):
        last = it == ITERS - 1
        if it == 0:
            arrived(atoms_b.at[0, pl.ds(0, lines - 1), 0], line_r.at[0])
            arrived(codes_main.at[0, :, :, pl.ds(0, width)], codes_r.at[0])
            codes_main[1, :, :, pl.ds(half, width)] = codes_main[0, :, :, pl.ds(0, width)]
        atoms = atoms_b[it, :, chip].reshape(lines * rows, lag_count)
        pair = jnp.concatenate([atoms[:, :half], atoms[:, half:]], axis=0)

        def correlate(at):
            picked = pl.ds(at, min(chunk, length - at))
            lagged[:, picked] = lax.dot_general(
                pair, codes_main[:, :, :, picked].reshape(2 * lines * rows, picked.size),
                (((0,), (0,)), ((), ())), preferred_element_type=F32,
            )

        correlate(0)
        for at in range(0, whole, chunk):
            if at + chunk < length:
                correlate(at + chunk)
            span = pl.ds(at, min(chunk, whole - at))
            shares[it, pos, :, span] = extended_ref[0, :, span] - factor * skew_total(lagged, at, span.size)
            if at // chunk % 2 == 0:
                continue
            held = shares.at[it, pos, :, pl.ds(at - chunk, chunk + span.size)]
            for bits in (7, 6, 3, 2, 5, 4, 1):
                start(copy_to(held, held, 2, halo_r.at[it, 0], member(flipped(bits))))
            if at == chunk:
                for to in range(team):
                    start(
                        copy_to(
                            shares.at[it, pos, :, pl.ds(0, lag_count)], from_following.at[it, pos],
                            2, halo_r.at[it, 2], member(to, group - 1),
                        ),
                        group > 0,
                    )
        for to in range(team):
            start(
                copy_to(
                    shares.at[it, pos, :, pl.ds(width, lag_count)], from_previous.at[it, pos],
                    2, halo_r.at[it, 1], member(to, group + 1),
                ),
                group < lines - 1,
            )
        if it == 0:
            for mate in mates:
                start(copy_to(rest.at[group], rest.at[group], 0, line_r.at[1], member(pos, mate)))
        for p in range(early, pieces) if it else ():
            share_atoms(it, p)

        @pl.when(group == 0)
        def _():
            from_previous[it] = jnp.zeros_like(from_previous[it])

        @pl.when(group == lines - 1)
        def _():
            from_following[it] = jnp.zeros_like(from_following[it])

        if it == 1:
            for bits in (6, 2, 4):
                wait_full(0, bits)
            arrived(codes_b, codes_r.at[1])
            for i in range(lines):
                for side in range(2):
                    advance(0, side, (i, slice(None)), team // 2)

        arrived(shares.at[it, pl.ds(0, team - 1)], halo_r.at[it, 0])
        pl.when(group > 0)(functools.partial(arrived, from_previous.at[it], halo_r.at[it, 1]))
        pl.when(group < lines - 1)(functools.partial(arrived, from_following.at[it], halo_r.at[it, 2]))
        total, head, tail = shares[it, 0], from_previous[it, 0], from_following[it, 0]
        for at in range(1, team):
            total, head, tail = total + shares[it, at], head + from_previous[it, at], tail + from_following[it, at]
        residual = jnp.concatenate(
            [total[:, :lag_count] + head, total[:, lag_count:width], total[:, width:] + tail], axis=1
        )
        lane = lax.broadcasted_iota(jnp.int32, residual.shape, 1)
        known = width + lag_count * jnp.minimum(lines - 1 - group, 1)
        residual = jnp.where(lane < known, residual, 0.0)
        if last:
            extended_ref[1] = residual
            residual_store = pltpu.make_async_copy(extended_ref.at[1, :, lanes_of(pos)], residual_out, local_sem.at[1])
            residual_store.start()
        residual = residual.astype(BF16).astype(F32)
        fill_frames(frames, residual, 0, length)

        def term(i, side):
            codes = codes_main[0, :, :, pl.ds(i * half, half)].reshape(lines * rows, half)
            return jnp.dot(codes, frames[:, pl.ds((i + side) * half, half)], preferred_element_type=F32)

        for side in range(2):
            if not last:
                outgoing = ready([
                    copy_to(sum_send.at[it, side], sum_recv.at[group, side], 3, sum_r.at[0], member(pos, mate))
                    for mate in mates
                ])
            else:
                outgoing = ready([
                    copy_to(sum_send.at[it, side, mate], last_recv.at[group, side], 3, sum_r.at[1], member(pos, mate))
                    for mate in mates
                ])

            @step
            def _():
                total = None
                for i in range(width // half):
                    total = term(i, side) if total is None else total + term(i, side)
                grad[:, :, pl.ds(side * half, half)] = total.reshape(lines, rows, half)
                sum_send[it, side] = total.reshape(lines, rows, half).astype(BF16)
                for copy in outgoing:
                    copy.start()

        if not last:
            for p in range(pieces) if it == 0 else ():
                share_atoms(0, p)
            step(functools.partial(advance_main, it))
            arrived(rest.at[pl.ds(0, lines - 1)], line_r.at[1])
            for mate in mates:
                atoms_ref[mate] = atoms_b[0, mate, chip].astype(F32) + rest[mate].astype(F32)
            arrived(sum_recv.at[pl.ds(0, lines - 1)], sum_r.at[0])
            total = grad[...]
            for mate in mates:
                theirs = jnp.concatenate([sum_recv[mate, 0], sum_recv[mate, 1]], axis=2)
                total = total + theirs.astype(F32)
            updated = atoms_ref[...] + factor * total
            fresh = updated / jnp.sqrt(jnp.mean(updated * updated, axis=2, keepdims=True) + EPSILON)
            atoms_ref[...] = fresh
            atoms_b[it + 1, :, chip] = fresh.astype(BF16)
            for p in range(early):
                share_atoms(it + 1, p)
            continue

        for bits in (0, 2, 4, 6):
            at = flipped(bits) // 2
            if bits:
                wait_full(it, bits)
            gives = ready([
                copy_to(
                    codes_b.at[:, at, :, lanes_of(1 - core)], codes_out.at[:, at, core], 1, out_r.at[0], partner
                )
            ])

            @step
            def _():
                advance(it, 1 - core, (slice(None), at), lines)
                gives[0].start()

            @step
            def _():
                advance(it, core, (slice(None), at), lines)
                held = codes_b.at[:, at, :, lanes_of(core)]
                pltpu.make_async_copy(held, codes_out.at[:, at, core], local_sem.at[0]).start()

        arrived(last_recv.at[pl.ds(0, lines - 1)], sum_r.at[1])
        total = grad[group]
        for mate in mates:
            total = total + jnp.concatenate([last_recv[mate, 0], last_recv[mate, 1]], axis=1).astype(F32)
        updated = atoms_ref[group] + factor * total
        atoms_out[...] = updated / jnp.sqrt(jnp.mean(updated * updated, axis=1, keepdims=True) + EPSILON)

    arrived(codes_out.at[:, :, 1 - core], out_r.at[0])
    arrived(codes_out.at[:, :, core], local_sem.at[0])
    residual_store.wait()
    for copy, when in sent:
        if when is None:
            copy.wait_send()
        else:
            pl.when(when)(copy.wait_send)


def on_device(n, signal, codes, dictionary, thresholds):
    _, atom_count, time_len = codes.shape
    rows, lag_count = dictionary.shape
    lines, team = n // 8, 8
    width, half = team * time_len, lag_count // 2
    vmem, dma = pltpu.VMEM, pltpu.SemaphoreType.DMA
    outside = pl.BlockSpec(memory_space=pltpu.HBM)
    piece = (rows, lag_count)
    split = (lines, 4, 2, rows, time_len)
    given = [
        pltpu.with_memory_space_constraint(x, pltpu.HBM)
        for x in (signal, codes.reshape(split), dictionary, thresholds[None, :])
    ]
    made = tuple(
        pl.pallas_call(
            functools.partial(kernel, n),
            name="learn",
            out_shape=(vmem(split, BF16), vmem(piece, F32), vmem(signal.shape, F32)),
            in_specs=[outside] * 4,
            out_specs=[pl.BlockSpec(memory_space=space) for space in (pl.ANY, pltpu.VMEM, pl.ANY)],
            scratch_shapes=[
                vmem((lines, *piece), F32),
                vmem((lines, *piece), BF16),
                vmem(signal.shape, F32),
                vmem((1, atom_count), F32),
                vmem((atom_count, 1), F32),
                vmem((lines, 4, rows, 1), F32),
                vmem((lines, 4, rows, 2 * time_len), BF16),
                vmem((lines, 4, rows, 2 * time_len), F32),
                vmem((ITERS, lines, 4, *piece), BF16),
                vmem((2, lines, rows, width + half), BF16),
                vmem((half, width + half), F32),
                vmem((half, width + half), BF16),
                vmem((lines, *piece), F32),
                vmem((2, 1, width + lag_count), F32),
                vmem((ITERS, team, 1, width + lag_count), F32),
                vmem((ITERS, team, 1, lag_count), F32),
                vmem((ITERS, team, 1, lag_count), F32),
                vmem((ITERS, 2, lines, rows, half), BF16),
                vmem((lines, 2, lines, rows, half), BF16),
                vmem((lines, 2, rows, half), BF16),
                dma((3,)),
                dma((4,)),
                dma((2,)),
                dma((ITERS, 3)),
                dma((2,)),
                dma((2,)),
                dma((ITERS, 3)),
                dma((1,)),
            ],
            compiler_params=pltpu.CompilerParams(
                collective_id=0, has_side_effects=True, vmem_limit_bytes=48_000_000
            ),
        )(*given)
    )

    def publish(codes_ref, atoms_ref, residual_ref, codes_out, atoms_out, residual_out, sems):
        pairs = [(codes_ref.at[:, i], codes_out.at[:, i]) for i in range(codes_ref.shape[1])]
        pairs += [(atoms_ref, atoms_out), (residual_ref, residual_out)]
        puts = [pltpu.make_async_copy(src, dst, sems.at[i]) for i, (src, dst) in enumerate(pairs)]
        for put in puts:
            put.start()
        for put in puts:
            put.wait()

    codes_out, atoms_out, residual_out = pl.pallas_call(
        publish,
        name="publish",
        out_shape=tuple(jax.ShapeDtypeStruct(x.shape, x.dtype) for x in made),
        in_specs=[pl.BlockSpec(memory_space=pl.ANY)] * 3,
        out_specs=(outside,) * 3,
        scratch_shapes=[dma((6,))],
        compiler_params=pltpu.CompilerParams(vmem_limit_bytes=1_000_000),
    )(*made)
    return codes_out.reshape(codes.shape), atoms_out, residual_out


def solution(mesh):
    return jax.shard_map(
        functools.partial(on_device, mesh.shape["tm"]),
        mesh=mesh,
        in_specs=(P("groups", "tm"), P("groups", None, "tm"), P("tm", None), P()),
        out_specs=(P("groups", None, "tm"), P(("groups", "tm"), None), P("groups", "tm")),
        check_vma=False,
    )
```
